32 devices in a mesh: dp: 8 (over y, x, core), opt: 4 (over z).
Axes of the slice: x: 2, y: 2, z: 4, core: 2. Of those that a mesh axis runs over, the one named last changes fastest.
Arguments:
- tokens: bfloat16 [64, 197, 384], P(('dp', 'opt')), may hold values from -6 to 6
- cotangent: bfloat16 [64, 197, 384], P(('dp', 'opt')), may hold values from -6 to 6
- w_qkv: float32 [384, 1152], P('opt'), may hold values from -1.5 to 1.5
- w_proj: float32 [384, 384], P('opt'), may hold values from -1.25 to 1.25
- w_fc1: float32 [384, 1536], P('opt'), may hold values from -0.3125 to 0.3125
- w_fc2: float32 [1536, 384], P('opt'), may hold values from -0.15625 to 0.15625
- vectors: float32 [12, 384], P('opt'), may hold values from -1 to 1.5
- mom_qkv: float32 [384, 1152], P('opt'), may hold values from -2.5 to 2.5
- mom_proj: float32 [384, 384], P('opt'), may hold values from -2.5 to 2.5
- mom_fc1: float32 [384, 1536], P('opt'), may hold values from -2.5 to 2.5
- mom_fc2: float32 [1536, 384], P('opt'), may hold values from -2.5 to 2.5
- mom_vectors: float32 [12, 384], P('opt'), may hold values from -2.5 to 2.5
Outputs:
- outputs: bfloat16 [64, 197, 384], P(('dp', 'opt'))
- grad_tokens: bfloat16 [64, 197, 384], P(('dp', 'opt'))
- grad_qkv: float32 [384, 1152], P('opt')
- grad_proj: float32 [384, 384], P('opt')
- grad_fc1: float32 [384, 1536], P('opt')
- grad_fc2: float32 [1536, 384], P('opt')
- grad_vectors: float32 [12, 384], P('opt')
- new_qkv: float32 [384, 1152], P('opt')
- new_proj: float32 [384, 384], P('opt')
- new_fc1: float32 [384, 1536], P('opt')
- new_fc2: float32 [1536, 384], P('opt')
- new_vectors: float32 [12, 384], P('opt')
- new_mom_qkv: float32 [384, 1152], P('opt')
- new_mom_proj: float32 [384, 384], P('opt')
- new_mom_fc1: float32 [384, 1536], P('opt')
- new_mom_fc2: float32 [1536, 384], P('opt')
- new_mom_vectors: float32 [12, 384], P('opt')
The draws below stay inside these ranges and needn't reach their ends.
All inputs are finite; a program needn't handle non-finite values.
Results may differ from the reference program's by a relative error of at most 0.022.
Values may be sent and summed in bfloat16 or wider, within the bound.
A program may use at most 128 MiB of HBM per device.

```python
import math
import jax
import jax.numpy as jnp
from jax import lax

D = 384
HEAD_DIM = 64
FF = 1536
SEQ = 197
IMG_DEV = 2
NS_ITERS = 5
IMAGES = 64
VEC_ROWS = 12
N_DP = 8
N_OPT = 4


def draw_w_qkv(key, part):
    base = jax.random.truncated_normal(key, -4.0, 4.0, (D, 3 * D), jnp.float32) * D ** (-0.5)
    return base


def draw_vectors(key, part):
    row_ids = jnp.arange(VEC_ROWS)[:, None] + jnp.zeros((VEC_ROWS, D), jnp.int32)
    is_gain = (row_ids == 0) | (row_ids == 5)
    noise = jax.random.truncated_normal(key, -4.0, 4.0, (VEC_ROWS, D), jnp.float32)
    gains = 1.0 + 0.1 * noise
    biases = 0.2 * noise
    return jnp.where(is_gain, gains, biases)


def block_levels(key, dims, pieces, smallest, largest):
    factor_of = 1.0
    for dim, shards_of in pieces:
        draws = jax.random.uniform(jax.random.fold_in(jax.random.fold_in(key, 6), dim), (shards_of,), jnp.float32, smallest / len(pieces), largest / len(pieces))
        factor_of = factor_of * jnp.repeat(jnp.exp(draws), dims[dim] // shards_of).reshape((-1,) + (1,) * (len(dims) - 1 - dim))
    return factor_of


def gaussian(own_key, dims, width, most, pieces=(), dtype=jnp.bfloat16):
    drawn = jax.random.normal(own_key, dims, jnp.float32) * width
    if len(pieces) > 0:
        drawn = block_levels(own_key, dims, pieces, -0.22, 0.18) * drawn
    return jnp.clip(drawn, min=-most, max=most).astype(dtype)


def setup_inputs(seed: int = 0) -> dict:
    seeds = jax.random.split(jax.random.key(seed), 13)
    return {
        "tokens": gaussian(seeds[0], (IMAGES, SEQ, D), 1.0, 6.0, ((0, 32),)),
        "cotangent": gaussian(seeds[1], (IMAGES, SEQ, D), 1.0, 6.0, ((0, 32),)),
        "w_qkv": draw_w_qkv(jax.random.fold_in(seeds[12], 71), 0),
        "w_proj": gaussian(seeds[3], (D, D), (D // 16) ** -0.5, 1.25, ((0, 4),), jnp.float32),
        "w_fc1": gaussian(seeds[4], (D, FF), D ** -0.5, 0.3125, ((0, 4),), jnp.float32),
        "w_fc2": gaussian(seeds[5], (FF, D), FF ** -0.5, 0.15625, ((0, 4),), jnp.float32),
        "vectors": draw_vectors(jax.random.fold_in(seeds[12], 71), 0),
        "mom_qkv": gaussian(seeds[7], (D, 3 * D), 0.2, 2.5, ((0, 4),), jnp.float32),
        "mom_proj": gaussian(seeds[8], (D, D), 0.2, 2.5, ((0, 4),), jnp.float32),
        "mom_fc1": gaussian(seeds[9], (D, FF), 0.2, 2.5, ((0, 4),), jnp.float32),
        "mom_fc2": gaussian(seeds[10], (FF, D), 0.2, 2.5, ((0, 4),), jnp.float32),
        "mom_vectors": gaussian(seeds[11], (VEC_ROWS, D), 0.3, 2.5, ((0, 4),), jnp.float32),
    }


NORM_EPSILON = 1e-06
MOMENTUM_DECAY = 0.9
VECTOR_RATE = 0.2
MATRIX_FACTOR = 0.04
COEF_FIRST = 3.4445
COEF_SECOND = -4.775
COEF_THIRD = 2.0315
ROOT_HALF = 0.7071067811865476
INV_ROOT_TAU = 0.3989422804014327

def contract(form, left, right):
    return jnp.einsum(form, left.astype(jnp.float32), right.astype(jnp.float32))

def norm_rows(values):
    row_mean = lax.optimization_barrier(jnp.mean(values, -1, keepdims=True))
    centered = values - row_mean
    inv_std = lax.rsqrt(lax.optimization_barrier(jnp.mean(centered * centered, -1, keepdims=True)) + NORM_EPSILON)
    return (centered * inv_std, inv_std)

def norm_back(grad_norm, normed, inv_std):
    return inv_std * (grad_norm - lax.optimization_barrier(jnp.mean(grad_norm, -1, keepdims=True)) - normed * lax.optimization_barrier(jnp.mean(grad_norm * normed, -1, keepdims=True)))

def layer_block(inputs, cotangent, w_qkv, w_proj, w_fc1, w_fc2, vectors):
    batch_size, seq_len, model_width = inputs.shape
    head_count = model_width // HEAD_DIM
    score_scale = HEAD_DIM ** (-0.5)
    vector_rows = vectors.astype(jnp.float32)
    gain_one = vector_rows[0]
    bias_one = vector_rows[1]
    bias_query = vector_rows[2]
    bias_value = vector_rows[3]
    bias_proj = vector_rows[4]
    gain_two = vector_rows[5]
    bias_two = vector_rows[6]
    bias_out = vector_rows[7]
    bias_hidden = vector_rows[8:].reshape(-1)

    def split_heads(block):
        return block.reshape(batch_size, seq_len, head_count, HEAD_DIM)
    flat_rows = inputs.reshape(-1, model_width).astype(jnp.float32)
    normed_one, inv_one = norm_rows(flat_rows)
    act_one = (normed_one * gain_one + bias_one).astype(jnp.bfloat16)
    qkv_rows = jnp.dot(act_one, w_qkv, preferred_element_type=jnp.float32)
    queries = (qkv_rows[:, :model_width] + bias_query).astype(jnp.bfloat16)
    key_rows = qkv_rows[:, model_width:2 * model_width].astype(jnp.bfloat16)
    values = (qkv_rows[:, 2 * model_width:] + bias_value).astype(jnp.bfloat16)
    query_heads = split_heads(queries)
    key_heads = split_heads(key_rows)
    value_heads = split_heads(values)
    scores = contract('bqhd,bkhd->bhqk', query_heads, key_heads) * score_scale
    row_top = lax.optimization_barrier(jnp.max(scores, -1, keepdims=True))
    log_total = row_top + jnp.log(lax.optimization_barrier(jnp.sum(jnp.exp(scores - row_top), -1, keepdims=True)))
    attn_probs = jnp.exp(scores - log_total)
    probs_low = attn_probs.astype(jnp.bfloat16)
    attended = contract('bhqk,bkhd->bqhd', probs_low, value_heads).astype(jnp.bfloat16).reshape(-1, model_width)
    middle = flat_rows + jnp.dot(attended, w_proj, preferred_element_type=jnp.float32) + bias_proj
    normed_two, inv_two = norm_rows(middle)
    act_two = (normed_two * gain_two + bias_two).astype(jnp.bfloat16)
    hidden_pre = jnp.dot(act_two, w_fc1, preferred_element_type=jnp.float32) + bias_hidden
    normal_cdf = 0.5 * (1.0 + lax.erf(hidden_pre * ROOT_HALF))
    hidden = (hidden_pre * normal_cdf).astype(jnp.bfloat16)
    result_rows = middle + jnp.dot(hidden, w_fc2, preferred_element_type=jnp.float32) + bias_out
    outputs = result_rows.astype(jnp.bfloat16).reshape(inputs.shape)
    grad_low = cotangent.reshape(-1, model_width)
    grad_out = grad_low.astype(jnp.float32)
    grad_fc2 = contract('rf,rd->fd', hidden, grad_low)
    slope = normal_cdf + hidden_pre * jnp.exp(-0.5 * hidden_pre * hidden_pre) * INV_ROOT_TAU
    grad_pre = jnp.dot(grad_low, w_fc2.T, preferred_element_type=jnp.float32) * slope
    pre_low = grad_pre.astype(jnp.bfloat16)
    grad_fc1 = contract('rd,rf->df', act_two, pre_low)
    grad_act_two = jnp.dot(pre_low, w_fc1.T, preferred_element_type=jnp.float32)
    grad_middle = grad_out + norm_back(grad_act_two * gain_two, normed_two, inv_two)
    middle_low = grad_middle.astype(jnp.bfloat16)
    grad_proj = contract('rd,re->de', attended, middle_low)
    grad_att = jnp.dot(middle_low, w_proj.T, preferred_element_type=jnp.float32).astype(jnp.bfloat16)
    att_heads = split_heads(grad_att)
    scores_again = contract('bqhd,bkhd->bhqk', query_heads, key_heads) * score_scale
    probs_again = jnp.exp(scores_again - log_total)
    again_low = probs_again.astype(jnp.bfloat16)
    grad_value = contract('bhqk,bqhd->bkhd', again_low, att_heads).reshape(-1, model_width)
    grad_probs = contract('bqhd,bkhd->bhqk', att_heads, value_heads)
    row_dot = lax.optimization_barrier(jnp.sum(probs_again * grad_probs, -1, keepdims=True))
    grad_scores = (probs_again * (grad_probs - row_dot) * score_scale).astype(jnp.bfloat16)
    grad_query = contract('bhqk,bkhd->bqhd', grad_scores, key_heads).reshape(-1, model_width)
    grad_key = contract('bhqk,bqhd->bkhd', grad_scores, query_heads).reshape(-1, model_width)
    qkv_low = jnp.concatenate([grad_query, grad_key, grad_value], 1).astype(jnp.bfloat16)
    grad_qkv = contract('rd,re->de', act_one, qkv_low)
    grad_act_one = jnp.dot(qkv_low, w_qkv.T, preferred_element_type=jnp.float32)
    grad_rows = grad_middle + norm_back(grad_act_one * gain_one, normed_one, inv_one)
    grad_tokens = grad_rows.astype(jnp.bfloat16).reshape(inputs.shape)
    small_rows = jnp.stack([lax.optimization_barrier(jnp.sum(grad_act_one * normed_one, 0)), lax.optimization_barrier(jnp.sum(grad_act_one, 0)), lax.optimization_barrier(jnp.sum(grad_query, 0)), lax.optimization_barrier(jnp.sum(grad_value, 0)), lax.optimization_barrier(jnp.sum(grad_middle, 0)), lax.optimization_barrier(jnp.sum(grad_act_two * normed_two, 0)), lax.optimization_barrier(jnp.sum(grad_act_two, 0)), lax.optimization_barrier(jnp.sum(grad_out, 0))])
    grad_vectors = jnp.concatenate([small_rows, lax.optimization_barrier(jnp.sum(grad_pre, 0)).reshape(-1, model_width)], 0)
    return (outputs, grad_tokens, (grad_qkv, grad_proj, grad_fc1, grad_fc2, grad_vectors))

def newton(matrix):
    row_count, col_count = matrix.shape
    highest = lax.Precision.HIGHEST
    ortho = matrix / (jnp.sqrt(jnp.sum(matrix * matrix)) + 1e-07)
    if row_count > col_count:
        ortho = ortho.T
    for sweep in range(NS_ITERS):
        gram_matrix = jnp.dot(ortho, ortho.T, precision=highest)
        poly_term = COEF_SECOND * gram_matrix + COEF_THIRD * jnp.dot(gram_matrix, gram_matrix, precision=highest)
        ortho = COEF_FIRST * ortho + jnp.dot(poly_term, ortho, precision=highest)
    if row_count > col_count:
        ortho = ortho.T
    return ortho * (MATRIX_FACTOR * math.sqrt(max(row_count, col_count)))

def reference(tokens, cotangent, w_qkv, w_proj, w_fc1, w_fc2, vectors, mom_qkv, mom_proj, mom_fc1, mom_fc2, mom_vectors):
    weights_low = (w_qkv.astype(jnp.bfloat16), w_proj.astype(jnp.bfloat16), w_fc1.astype(jnp.bfloat16), w_fc2.astype(jnp.bfloat16), vectors.astype(jnp.bfloat16))
    group_size = IMG_DEV * N_OPT
    token_blocks = tokens.reshape(N_DP, group_size, SEQ, D)
    cot_blocks = cotangent.reshape(N_DP, group_size, SEQ, D)

    def block_step(carry, block_pair):
        block_out, block_grad, block_terms = layer_block(block_pair[0], block_pair[1], *weights_low)
        return (jax.tree.map(lambda left, right: left + right, carry, block_terms), (block_out, block_grad))
    start_sums = (jnp.zeros((D, 3 * D), jnp.float32), jnp.zeros((D, D), jnp.float32), jnp.zeros((D, FF), jnp.float32), jnp.zeros((FF, D), jnp.float32), jnp.zeros((VEC_ROWS, D), jnp.float32))
    grad_sums, stacked = lax.scan(block_step, start_sums, (token_blocks, cot_blocks))
    outputs = stacked[0].reshape(IMAGES, SEQ, D)
    grad_tokens = stacked[1].reshape(IMAGES, SEQ, D)
    grad_scale = 1.0 / math.sqrt(IMAGES * SEQ)
    old_moms = (mom_qkv, mom_proj, mom_fc1, mom_fc2, mom_vectors)
    new_moms = tuple((MOMENTUM_DECAY * old_state + grad_part * grad_scale for old_state, grad_part in zip(old_moms, grad_sums)))
    new_mats = tuple((weight_now - newton(moment) for weight_now, moment in zip((w_qkv, w_proj, w_fc1, w_fc2), new_moms[:4])))
    vector_mom = new_moms[4]
    new_vectors = vectors - VECTOR_RATE * vector_mom * lax.rsqrt(lax.optimization_barrier(jnp.mean(vector_mom * vector_mom, -1, keepdims=True)) + NORM_EPSILON)
    return (outputs, grad_tokens, grad_sums[0], grad_sums[1], grad_sums[2], grad_sums[3], grad_sums[4], new_mats[0], new_mats[1], new_mats[2], new_mats[3], new_vectors, new_moms[0], new_moms[1], new_moms[2], new_moms[3], new_moms[4])
```

```python
import functools
import math

import jax
import jax.numpy as jnp
from jax import lax
from jax.experimental import pallas as pl
from jax.experimental.pallas import tpu as pltpu
from jax.sharding import PartitionSpec as P

HEAD_DIM = 64
NS_ITERS = 5


NORM_EPSILON = 1e-06
MOMENTUM_DECAY = 0.9
VECTOR_RATE = 0.2
MATRIX_FACTOR = 0.04
COEF_FIRST = 3.4445
COEF_SECOND = -4.775
COEF_THIRD = 2.0315
ROOT_HALF = 0.7071067811865476
INV_ROOT_TAU = 0.3989422804014327

MESH = pl.DeviceIdType.MESH
BF16 = jnp.bfloat16
F32 = jnp.float32


class Plan:
    def __init__(self, n_dp, n_opt):
        self.n_dp, self.n_opt = n_dp, n_opt
        self.me = lax.axis_index("opt")
        dp = lax.axis_index("dp")
        self.dp = dp
        self.stages = n_dp.bit_length() - 1
        bits = [lax.rem(lax.div(dp, jnp.int32(2**p)), jnp.int32(2)) for p in range(self.stages)]
        core = bits[0]
        self.bit, self.partner, self.base = [], [], [jnp.int32(0)]
        for t in range(self.stages):
            up = t
            down = 0 if t == 0 else self.stages - t
            bit = bits[up] + core * (bits[down] - bits[up]) if t else bits[0]
            weight = 2**up + core * (2**down - 2**up) if t else 1
            self.bit.append(bit)
            self.partner.append(dp + weight * (1 - 2 * bit))
            self.base.append(self.base[-1] + bit * (n_dp >> (t + 1)))
        self.chunk = self.base[-1]

    def peer(self, j):
        return lax.rem(self.me + j, jnp.int32(self.n_opt))

    def barrier(self):
        sem = pltpu.get_barrier_semaphore()
        for t in range(self.stages):
            pl.semaphore_signal(
                sem, inc=1, device_id=(self.partner[t], self.me), device_id_type=MESH
            )
        for j in range(1, self.n_opt):
            pl.semaphore_signal(
                sem, inc=1, device_id=(self.dp, self.peer(j)), device_id_type=MESH
            )
        pl.semaphore_wait(sem, self.stages + self.n_opt - 1)

    def to_partner(self, t, src, dst, send, recv):
        return pltpu.make_async_remote_copy(
            src_ref=src, dst_ref=dst, send_sem=send, recv_sem=recv,
            device_id=(self.partner[t], self.me), device_id_type=MESH,
        )

    def to_peer(self, j, src, dst, send, recv):
        return pltpu.make_async_remote_copy(
            src_ref=src, dst_ref=dst, send_sem=send, recv_sem=recv,
            device_id=(self.dp, self.peer(j)), device_id_type=MESH,
        )


def gather_weights_kernel(n_dp, n_opt, w_ref, v_ref, out_ref, vout_ref, zs, zr, vs, vr, gs, gr):
    plan = Plan(n_dp, n_opt)
    me, cid = plan.me, plan.chunk
    out_ref[me, :, cid] = w_ref[:, cid]
    vout_ref[me] = v_ref[...]
    plan.barrier()
    flights = []
    hops = []
    for j in range(1, n_opt):
        copy = plan.to_peer(
            j, w_ref.at[:, cid], out_ref.at[me, :, cid], zs.at[j], zr.at[j]
        )
        copy.start()
        hops.append(copy)
        small = plan.to_peer(j, v_ref, vout_ref.at[me], vs.at[j], vr.at[j])
        small.start()
        flights.append(small)
    for t in reversed(range(plan.stages)):
        count = n_dp >> (t + 1)
        for j in range(n_opt):
            q = plan.peer(n_opt - j)
            if t == plan.stages - 1:
                if j > 0:
                    hops[j - 1].wait_recv()
            else:
                pending[j].wait_recv()
            where = out_ref.at[q, :, pl.ds(plan.base[t + 1], count)]
            copy = plan.to_partner(t, where, where, gs.at[t, j], gr.at[t, j])
            copy.start()
            if j == 0:
                fresh = []
            fresh.append(copy)
        pending = fresh
        flights.append(fresh)
    for copy in pending:
        copy.wait_recv()
    for copy in hops:
        copy.wait_send()
    for entry in flights:
        if isinstance(entry, list):
            for copy in entry:
                copy.wait_send()
        else:
            entry.wait()


def gather_weights(packed, small, n_dp, n_opt):
    groups, _, rows, width = packed.shape
    stages = n_dp.bit_length() - 1
    dma = pltpu.SemaphoreType.DMA
    return pl.pallas_call(
        functools.partial(gather_weights_kernel, n_dp, n_opt),
        out_shape=(
            jax.ShapeDtypeStruct((n_opt,) + packed.shape, packed.dtype),
            jax.ShapeDtypeStruct((n_opt,) + small.shape, small.dtype),
        ),
        in_specs=[pl.BlockSpec(memory_space=pltpu.VMEM)] * 2,
        out_specs=[pl.BlockSpec(memory_space=pltpu.VMEM)] * 2,
        scratch_shapes=[
            dma((n_opt,)), dma((n_opt,)), dma((n_opt,)), dma((n_opt,)),
            dma((stages, n_opt)), dma((stages, n_opt)),
        ],
        compiler_params=pltpu.CompilerParams(
            collective_id=0, has_side_effects=True, vmem_limit_bytes=48 * 2**20
        ),
        name="gather_weights",
    )(packed, small)


def reduce_kernel(n_dp, n_opt, grad_scale, g_ref, v_ref, m_ref, out_ref, vout_ref, *rest):
    plan = Plan(n_dp, n_opt)
    me, cid = plan.me, plan.chunk
    stages = plan.stages
    got = rest[:stages]
    acc = rest[stages : 2 * stages]
    zgot, mo, vgot, vacc, vz, ss, sr, zs, zr, ms, mr, gs, gr, vs, vr, us, ur = rest[2 * stages :]
    plan.barrier()
    sends = []

    def launch(t, j):
        half = n_dp >> (t + 1)
        q = plan.peer(j + 1)
        other = (1 - plan.bit[t]) * half
        src = (g_ref if t == 0 else acc[t - 1]).at[q, :, pl.ds(other, half)]
        copy = plan.to_partner(t, src, got[t].at[j], ss.at[t, j], sr.at[t, j])
        copy.start()
        return copy

    def launch_small(t):
        copy = plan.to_partner(
            t, v_ref if t == 0 else vacc.at[t - 1], vgot.at[t], vs.at[t], vr.at[t]
        )
        copy.start()
        return copy

    vcopy = launch_small(0)
    current = [launch(0, j) for j in range(n_opt)]
    zcopies = []
    vz_copies = []
    for t in range(stages):
        half = n_dp >> (t + 1)
        following = []
        for j in range(n_opt):
            q = plan.peer(j + 1)
            current[j].wait_recv()
            sends.append(current[j])
            source = g_ref if t == 0 else acc[t - 1]
            mine = plan.bit[t] * half
            kept = source[q, :, pl.ds(mine, half)].astype(F32)
            acc[t][q] = (kept + got[t][j].astype(F32)).astype(BF16)
            if t + 1 < stages:
                following.append(launch(t + 1, j))
            elif j < n_opt - 1:
                copy = plan.to_peer(j + 1, acc[t].at[q, :, 0], zgot.at[j], zs.at[j], zr.at[j])
                copy.start()
                zcopies.append(copy)
        current = following
        vcopy.wait_recv()
        sends.append(vcopy)
        vacc[t] = (v_ref[...] if t == 0 else vacc[t - 1]) + vgot[t]
        if t + 1 < stages:
            vcopy = launch_small(t + 1)
        else:
            for j in range(n_opt - 1):
                copy = plan.to_peer(
                    j + 1, vacc.at[t, plan.peer(j + 1)], vz.at[j], us.at[j], ur.at[j]
                )
                copy.start()
                vz_copies.append(copy)
    total = acc[stages - 1][me, :, 0].astype(F32)
    for j in range(n_opt - 1):
        zcopies[j].wait_recv()
        total = total + zgot[j].astype(F32)
    out_ref[0:3, cid] = total.astype(BF16)
    mo[...] = (MOMENTUM_DECAY * m_ref[:, cid] + total * grad_scale).astype(BF16)
    mcopies = []
    for j in range(1, n_opt):
        group = jnp.maximum(plan.peer(j) - 1, 0)
        copy = plan.to_peer(j, mo.at[group], out_ref.at[3 + me, cid], ms.at[j], mr.at[j])
        copy.start()
        mcopies.append(copy)
    out_ref[3 + me, cid] = mo[jnp.maximum(me - 1, 0)]
    vtotal = vacc[stages - 1, me]
    for j in range(n_opt - 1):
        vz_copies[j].wait_recv()
        vtotal = vtotal + vz[j]
    vout_ref[...] = vtotal
    for copy in mcopies:
        copy.wait_recv()
    for t in reversed(range(stages)):
        where = out_ref.at[:, pl.ds(plan.base[t + 1], n_dp >> (t + 1))]
        copy = plan.to_partner(t, where, where, gs.at[t], gr.at[t])
        copy.start()
        copy.wait_recv()
        sends.append(copy)
    for copy in sends + zcopies + vz_copies + mcopies:
        copy.wait_send()


def reduce_grads(packed, small, moms, grad_scale, n_dp, n_opt):
    _, groups, _, rows, width = packed.shape
    stages = n_dp.bit_length() - 1
    dma = pltpu.SemaphoreType.DMA
    halves = [
        pltpu.VMEM((n_opt, groups, n_dp >> (t + 1), rows, width), BF16) for t in range(stages)
    ]
    return pl.pallas_call(
        functools.partial(reduce_kernel, n_dp, n_opt, grad_scale),
        out_shape=(
            jax.ShapeDtypeStruct((groups + n_opt, n_dp, rows, width), BF16),
            jax.ShapeDtypeStruct(small.shape[1:], F32),
        ),
        in_specs=[pl.BlockSpec(memory_space=pltpu.VMEM)] * 3,
        out_specs=[pl.BlockSpec(memory_space=pltpu.VMEM)] * 2,
        scratch_shapes=halves
        + halves
        + [
            pltpu.VMEM((n_opt - 1, groups, rows, width), BF16),
            pltpu.VMEM((groups, rows, width), BF16),
            pltpu.VMEM((stages,) + small.shape, F32),
            pltpu.VMEM((stages,) + small.shape, F32),
            pltpu.VMEM((n_opt - 1,) + small.shape[1:], F32),
            dma((stages, n_opt)), dma((stages, n_opt)),
            dma((n_opt,)), dma((n_opt,)), dma((n_opt,)), dma((n_opt,)),
            dma((stages,)), dma((stages,)), dma((stages,)), dma((stages,)),
            dma((n_opt,)), dma((n_opt,)),
        ],
        compiler_params=pltpu.CompilerParams(
            collective_id=1, has_side_effects=True, vmem_limit_bytes=56 * 2**20
        ),
        name="reduce_grads",
    )(packed, small, moms)


def spread_kernel(n_dp, n_opt, first_chunks, o_ref, out_ref, zgot, zs, zr, gs, gr):
    plan = Plan(n_dp, n_opt)
    me, cid = plan.me, plan.chunk
    zgot[me] = o_ref[me, cid]
    plan.barrier()
    copies = []
    for j in range(1, n_opt):
        copy = plan.to_peer(j, o_ref.at[plan.peer(j), cid], zgot.at[me], zs.at[j], zr.at[j])
        copy.start()
        copies.append(copy)
    for copy in copies:
        copy.wait_recv()
    late = lax.div(cid, jnp.int32(first_chunks))
    out_ref[0, cid] = zgot[jnp.minimum(late, 1)]
    out_ref[1, cid] = zgot[2]
    out_ref[2, cid] = zgot[3]
    for t in reversed(range(plan.stages)):
        where = out_ref.at[:, pl.ds(plan.base[t + 1], n_dp >> (t + 1))]
        copy = plan.to_partner(t, where, where, gs.at[t], gr.at[t])
        copy.start()
        copy.wait_recv()
        copies.append(copy)
    for copy in copies:
        copy.wait_send()


def spread_updates(ortho, first_chunks, n_dp, n_opt):
    _, _, rows, width = ortho.shape
    stages = n_dp.bit_length() - 1
    dma = pltpu.SemaphoreType.DMA
    return pl.pallas_call(
        functools.partial(spread_kernel, n_dp, n_opt, first_chunks),
        out_shape=jax.ShapeDtypeStruct((3, n_dp, rows, width), BF16),
        in_specs=[pl.BlockSpec(memory_space=pltpu.VMEM)],
        out_specs=pl.BlockSpec(memory_space=pltpu.VMEM),
        scratch_shapes=[
            pltpu.VMEM((n_opt, rows, width), BF16),
            dma((n_opt,)), dma((n_opt,)), dma((stages,)), dma((stages,)),
        ],
        compiler_params=pltpu.CompilerParams(
            collective_id=2, has_side_effects=True, vmem_limit_bytes=48 * 2**20
        ),
        name="spread_updates",
    )(ortho)


def pair(values):
    high = values.astype(BF16)
    return high, (values - high.astype(F32)).astype(BF16)


def dot_rows(left, right):
    return lax.dot_general(left, right, (((1,), (1,)), ((), ())), preferred_element_type=F32)


def dot_plain(left, right):
    return lax.dot_general(left, right, (((1,), (0,)), ((), ())), preferred_element_type=F32)


def newton_kernel(n_opt, m_ref, out_ref, y_ref):
    rank = lax.axis_index("opt")
    _, width, _ = m_ref.shape
    part = width // n_opt

    @pl.when(rank < 3)
    def _():
        for q in range(n_opt):
            for b in range(4):
                is_proj = b == 3
                keep = (rank == 2) | ((rank == 1) if is_proj else (rank == 0))
                block = m_ref[q, b * part : (b + 1) * part, :].astype(F32)
                y_ref[q * part : (q + 1) * part, b * width : (b + 1) * width] = (
                    block * keep.astype(F32)
                )

    @pl.when(rank == 3)
    def _():
        for q in range(n_opt):
            y_ref[:, q * width : (q + 1) * width] = m_ref[q].astype(F32).T

    start = y_ref[...]
    norm = jnp.sqrt(jnp.sum(jnp.sum(start * start, 1, keepdims=True), 0, keepdims=True)) + 1e-07
    y_ref[...] = start / norm

    def sweep(_, carry):
        ortho = y_ref[...]
        high, low = pair(ortho)
        cross = dot_rows(high, low)
        gram = dot_rows(high, high) + (cross + cross.T)
        gram_high, gram_low = pair(gram)
        twist = dot_plain(gram_high, gram_low)
        square = dot_plain(gram_high, gram_high) + (twist + twist.T)
        poly = COEF_SECOND * gram + COEF_THIRD * square
        poly_high, poly_low = pair(poly)
        y_ref[...] = COEF_FIRST * ortho + (
            dot_plain(poly_high, high) + (dot_plain(poly_high, low) + dot_plain(poly_low, high))
        )
        return carry

    lax.fori_loop(0, NS_ITERS, sweep, 0)
    wide = math.sqrt(n_opt * width)
    middle = math.sqrt(3 * width)
    factor = MATRIX_FACTOR * jnp.where(
        rank == 0, middle, jnp.where(rank == 1, math.sqrt(width), wide)
    ).astype(F32)

    @pl.when(rank < 3)
    def _():
        for q in range(n_opt):
            for b in range(4):
                block = y_ref[q * part : (q + 1) * part, b * width : (b + 1) * width]
                out_ref[q, b * part : (b + 1) * part, :] = (block * factor).astype(BF16)

    @pl.when(rank == 3)
    def _():
        for q in range(n_opt):
            out_ref[q] = (y_ref[:, q * width : (q + 1) * width].T * factor).astype(BF16)


def newton_owned(mats):
    n_opt, width, _ = mats.shape
    return pl.pallas_call(
        functools.partial(newton_kernel, n_opt),
        out_shape=jax.ShapeDtypeStruct(mats.shape, BF16),
        in_specs=[pl.BlockSpec(memory_space=pltpu.VMEM)],
        out_specs=pl.BlockSpec(memory_space=pltpu.VMEM),
        scratch_shapes=[pltpu.VMEM((width, n_opt * width), F32)],
        compiler_params=pltpu.CompilerParams(vmem_limit_bytes=48 * 2**20),
        name="newton_owned",
    )(mats)


def stack_blocks(matrix, width):
    return jnp.concatenate(
        [matrix[:, i : i + width] for i in range(0, matrix.shape[1], width)], 0
    )


def unstack_blocks(stacked, rows):
    return jnp.concatenate(
        [stacked[i : i + rows] for i in range(0, stacked.shape[0], rows)], 1
    )


def pack_rows(qkv, proj, fc1, fc2):
    width = proj.shape[1]
    return jnp.stack(
        [
            jnp.concatenate([stack_blocks(qkv, width), proj], 0),
            stack_blocks(fc1, width),
            fc2,
        ]
    )


def unpack_rows(packed, part):
    both = packed[0]
    return (
        unstack_blocks(both[: 3 * part], part),
        both[3 * part :],
        unstack_blocks(packed[1], part),
        packed[2],
    )


def contract(form, left, right):
    return jnp.einsum(form, left, right, preferred_element_type=jnp.float32)


def norm_rows(values):
    row_mean = jnp.mean(values, -1, keepdims=True)
    centered = values - row_mean
    inv_std = lax.rsqrt(jnp.mean(centered * centered, -1, keepdims=True) + NORM_EPSILON)
    return (centered * inv_std, inv_std)


def norm_back(grad_norm, normed, inv_std):
    return inv_std * (
        grad_norm
        - jnp.mean(grad_norm, -1, keepdims=True)
        - normed * jnp.mean(grad_norm * normed, -1, keepdims=True)
    )


def layer_block(inputs, cotangent, w_qkv, w_proj, w_fc1, w_fc2, vectors):
    batch_size, seq_len, model_width = inputs.shape
    head_count = model_width // HEAD_DIM
    score_scale = HEAD_DIM ** (-0.5)
    vector_rows = vectors.astype(jnp.float32)
    gain_one = vector_rows[0]
    bias_one = vector_rows[1]
    bias_query = vector_rows[2]
    bias_value = vector_rows[3]
    bias_proj = vector_rows[4]
    gain_two = vector_rows[5]
    bias_two = vector_rows[6]
    bias_out = vector_rows[7]
    bias_hidden = vector_rows[8:].reshape(-1)

    def split_heads(block):
        return block.reshape(batch_size, seq_len, head_count, HEAD_DIM)

    flat_rows = inputs.reshape(-1, model_width).astype(jnp.float32)
    normed_one, inv_one = norm_rows(flat_rows)
    act_one = (normed_one * gain_one + bias_one).astype(jnp.bfloat16)
    qkv_rows = jnp.dot(act_one, w_qkv, preferred_element_type=jnp.float32)
    queries = (qkv_rows[:, :model_width] + bias_query).astype(jnp.bfloat16)
    key_rows = qkv_rows[:, model_width : 2 * model_width].astype(jnp.bfloat16)
    values = (qkv_rows[:, 2 * model_width :] + bias_value).astype(jnp.bfloat16)
    query_heads = split_heads(queries)
    key_heads = split_heads(key_rows)
    value_heads = split_heads(values)
    scores = contract("bqhd,bkhd->bhqk", query_heads, key_heads) * score_scale
    row_top = jnp.max(scores, -1, keepdims=True)
    log_total = row_top + jnp.log(jnp.sum(jnp.exp(scores - row_top), -1, keepdims=True))
    attn_probs = jnp.exp(scores - log_total)
    probs_low = attn_probs.astype(jnp.bfloat16)
    attended = (
        contract("bhqk,bkhd->bqhd", probs_low, value_heads)
        .astype(jnp.bfloat16)
        .reshape(-1, model_width)
    )
    middle = flat_rows + jnp.dot(attended, w_proj, preferred_element_type=jnp.float32) + bias_proj
    normed_two, inv_two = norm_rows(middle)
    act_two = (normed_two * gain_two + bias_two).astype(jnp.bfloat16)
    hidden_pre = jnp.dot(act_two, w_fc1, preferred_element_type=jnp.float32) + bias_hidden
    normal_cdf = 0.5 * (1.0 + lax.erf(hidden_pre * ROOT_HALF))
    hidden = (hidden_pre * normal_cdf).astype(jnp.bfloat16)
    result_rows = middle + jnp.dot(hidden, w_fc2, preferred_element_type=jnp.float32) + bias_out
    outputs = result_rows.astype(jnp.bfloat16).reshape(inputs.shape)
    grad_low = cotangent.reshape(-1, model_width)
    grad_out = grad_low.astype(jnp.float32)
    grad_fc2 = contract("rf,rd->fd", hidden, grad_low)
    slope = normal_cdf + hidden_pre * jnp.exp(-0.5 * hidden_pre * hidden_pre) * INV_ROOT_TAU
    grad_pre = jnp.dot(grad_low, w_fc2.T, preferred_element_type=jnp.float32) * slope
    pre_low = grad_pre.astype(jnp.bfloat16)
    grad_fc1 = contract("rd,rf->df", act_two, pre_low)
    grad_act_two = jnp.dot(pre_low, w_fc1.T, preferred_element_type=jnp.float32)
    grad_middle = grad_out + norm_back(grad_act_two * gain_two, normed_two, inv_two)
    middle_low = grad_middle.astype(jnp.bfloat16)
    grad_proj = contract("rd,re->de", attended, middle_low)
    grad_att = jnp.dot(middle_low, w_proj.T, preferred_element_type=jnp.float32).astype(
        jnp.bfloat16
    )
    att_heads = split_heads(grad_att)
    scores_again = contract("bqhd,bkhd->bhqk", query_heads, key_heads) * score_scale
    probs_again = jnp.exp(scores_again - log_total)
    again_low = probs_again.astype(jnp.bfloat16)
    grad_value = contract("bhqk,bqhd->bkhd", again_low, att_heads).reshape(-1, model_width)
    grad_probs = contract("bqhd,bkhd->bhqk", att_heads, value_heads)
    row_dot = jnp.sum(probs_again * grad_probs, -1, keepdims=True)
    grad_scores = (probs_again * (grad_probs - row_dot) * score_scale).astype(jnp.bfloat16)
    grad_query = contract("bhqk,bkhd->bqhd", grad_scores, key_heads).reshape(-1, model_width)
    grad_key = contract("bhqk,bqhd->bkhd", grad_scores, query_heads).reshape(-1, model_width)
    qkv_low = jnp.concatenate([grad_query, grad_key, grad_value], 1).astype(jnp.bfloat16)
    grad_qkv = contract("rd,re->de", act_one, qkv_low)
    grad_act_one = jnp.dot(qkv_low, w_qkv.T, preferred_element_type=jnp.float32)
    grad_rows = grad_middle + norm_back(grad_act_one * gain_one, normed_one, inv_one)
    grad_tokens = grad_rows.astype(jnp.bfloat16).reshape(inputs.shape)
    small_rows = jnp.stack(
        [
            jnp.sum(grad_act_one * normed_one, 0),
            jnp.sum(grad_act_one, 0),
            jnp.sum(grad_query, 0),
            jnp.sum(grad_value, 0),
            jnp.sum(grad_middle, 0),
            jnp.sum(grad_act_two * normed_two, 0),
            jnp.sum(grad_act_two, 0),
            jnp.sum(grad_out, 0),
        ]
    )
    grad_vectors = jnp.concatenate([small_rows, jnp.sum(grad_pre, 0).reshape(-1, model_width)], 0)
    return (outputs, grad_tokens, (grad_qkv, grad_proj, grad_fc1, grad_fc2, grad_vectors))


def body(
    tokens,
    cotangent,
    w_qkv,
    w_proj,
    w_fc1,
    w_fc2,
    vectors,
    mom_qkv,
    mom_proj,
    mom_fc1,
    mom_fc2,
    mom_vectors,
):
    n_dp, n_opt = lax.axis_size("dp"), lax.axis_size("opt")
    part, width = w_proj.shape
    rows = width // n_dp
    small_count = vectors.shape[0]
    pad = -small_count % 8

    def cut(packed):
        return packed.reshape(packed.shape[:-2] + (n_dp, rows, width))

    def join(packed):
        return packed.reshape(packed.shape[:-3] + (width, width))

    weights_mine = cut(pack_rows(*[w.astype(BF16) for w in (w_qkv, w_proj, w_fc1, w_fc2)]))
    small_mine = jnp.pad(vectors.astype(BF16).astype(F32), ((0, pad), (0, 0)))
    all_weights, all_small = gather_weights(weights_mine, small_mine, n_dp, n_opt)
    all_weights = join(all_weights)
    full = [unpack_rows(all_weights[q], part) for q in range(n_opt)]
    whole = [jnp.concatenate([piece[i] for piece in full], 0) for i in range(4)]
    full_vectors = all_small[:, :small_count].reshape(-1, width)
    outputs, grad_tokens, partials = layer_block(tokens, cotangent, *whole, full_vectors)
    packed = cut(
        jnp.stack(
            [
                pack_rows(
                    *[
                        lax.slice_in_dim(p, q * (p.shape[0] // n_opt), (q + 1) * (p.shape[0] // n_opt)).astype(BF16)
                        for p in partials[:4]
                    ]
                )
                for q in range(n_opt)
            ]
        )
    )
    small = jnp.pad(partials[4].reshape(n_opt, small_count, width), ((0, 0), (0, pad), (0, 0)))
    token_total = tokens.shape[0] * tokens.shape[1] * n_dp * n_opt
    grad_scale = 1.0 / math.sqrt(token_total)
    moms = cut(pack_rows(mom_qkv, mom_proj, mom_fc1, mom_fc2))
    summed, small_sum = reduce_grads(packed, small, moms, grad_scale, n_dp, n_opt)
    summed = join(summed)
    shares = tuple(x.astype(F32) for x in unpack_rows(summed[:3], part)) + (
        small_sum[:small_count],
    )
    old_moms = (mom_qkv, mom_proj, mom_fc1, mom_fc2, mom_vectors)
    new_moms = tuple(
        (
            MOMENTUM_DECAY * old_state + share_part * grad_scale
            for old_state, share_part in zip(old_moms, shares)
        )
    )
    vector_mom = new_moms[4]
    new_vectors = vectors - VECTOR_RATE * vector_mom * lax.rsqrt(
        jnp.mean(vector_mom * vector_mom, -1, keepdims=True) + NORM_EPSILON
    )
    ortho = newton_owned(summed[3:])
    updates = join(spread_updates(cut(ortho), 3 * part // rows, n_dp, n_opt))
    new_mats = tuple(
        (
            weight_now - update_part.astype(F32)
            for weight_now, update_part in zip(
                (w_qkv, w_proj, w_fc1, w_fc2), unpack_rows(updates, part)
            )
        )
    )
    return (outputs, grad_tokens) + shares + new_mats + (new_vectors,) + new_moms


def solution(mesh):
    return jax.shard_map(
        body,
        mesh=mesh,
        in_specs=(
            P(("dp", "opt"), None, None),
            P(("dp", "opt"), None, None),
            P("opt", None),
            P("opt", None),
            P("opt", None),
            P("opt", None),
            P("opt", None),
            P("opt", None),
            P("opt", None),
            P("opt", None),
            P("opt", None),
            P("opt", None),
        ),
        out_specs=(
            P(("dp", "opt"), None, None),
            P(("dp", "opt"), None, None),
            P("opt", None),
            P("opt", None),
            P("opt", None),
            P("opt", None),
            P("opt", None),
            P("opt", None),
            P("opt", None),
            P("opt", None),
            P("opt", None),
            P("opt", None),
            P("opt", None),
            P("opt", None),
            P("opt", None),
            P("opt", None),
            P("opt", None),
        ),
        check_vma=False,
    )
```

```python
import functools
import math

import jax
import jax.numpy as jnp
from jax import lax
from jax.experimental import pallas as pl
from jax.experimental.pallas import tpu as pltpu
from jax.sharding import PartitionSpec as P

HEAD_DIM = 64
NS_ITERS = 5


NORM_EPSILON = 1e-06
MOMENTUM_DECAY = 0.9
VECTOR_RATE = 0.2
MATRIX_FACTOR = 0.04
COEF_FIRST = 3.4445
COEF_SECOND = -4.775
COEF_THIRD = 2.0315
ROOT_HALF = 0.7071067811865476
INV_ROOT_TAU = 0.3989422804014327

MESH = pl.DeviceIdType.MESH
BF16 = jnp.bfloat16
F32 = jnp.float32


class Plan:
    def __init__(self, n_dp, n_opt):
        self.n_dp, self.n_opt = n_dp, n_opt
        self.me = lax.axis_index("opt")
        dp = lax.axis_index("dp")
        self.dp = dp
        self.stages = n_dp.bit_length() - 1
        bits = [lax.rem(lax.div(dp, jnp.int32(2**p)), jnp.int32(2)) for p in range(self.stages)]
        core = bits[0]
        self.bit, self.partner, self.base = [], [], [jnp.int32(0)]
        for t in range(self.stages):
            up = t
            down = 0 if t == 0 else self.stages - t
            bit = bits[up] + core * (bits[down] - bits[up]) if t else bits[0]
            weight = 2**up + core * (2**down - 2**up) if t else 1
            self.bit.append(bit)
            self.partner.append(dp + weight * (1 - 2 * bit))
            self.base.append(self.base[-1] + bit * (n_dp >> (t + 1)))
        self.chunk = self.base[-1]

    def peer(self, j):
        return lax.rem(self.me + j, jnp.int32(self.n_opt))

    def barrier(self):
        sem = pltpu.get_barrier_semaphore()
        for t in range(self.stages):
            pl.semaphore_signal(
                sem, inc=1, device_id=(self.partner[t], self.me), device_id_type=MESH
            )
        for j in range(1, self.n_opt):
            pl.semaphore_signal(
                sem, inc=1, device_id=(self.dp, self.peer(j)), device_id_type=MESH
            )
        pl.semaphore_wait(sem, self.stages + self.n_opt - 1)

    def to_partner(self, t, src, dst, send, recv):
        return pltpu.make_async_remote_copy(
            src_ref=src, dst_ref=dst, send_sem=send, recv_sem=recv,
            device_id=(self.partner[t], self.me), device_id_type=MESH,
        )

    def to_peer(self, j, src, dst, send, recv):
        return pltpu.make_async_remote_copy(
            src_ref=src, dst_ref=dst, send_sem=send, recv_sem=recv,
            device_id=(self.dp, self.peer(j)), device_id_type=MESH,
        )


def gather_weights_kernel(n_dp, n_opt, w_ref, v_ref, out_ref, vout_ref, zs, zr, vs, vr, gs, gr):
    plan = Plan(n_dp, n_opt)
    me, cid = plan.me, plan.chunk
    out_ref[me, :, cid] = w_ref[:, cid]
    vout_ref[me] = v_ref[...]
    plan.barrier()
    flights = []
    hops = []
    for j in range(1, n_opt):
        copy = plan.to_peer(
            j, w_ref.at[:, cid], out_ref.at[me, :, cid], zs.at[j], zr.at[j]
        )
        copy.start()
        hops.append(copy)
        small = plan.to_peer(j, v_ref, vout_ref.at[me], vs.at[j], vr.at[j])
        small.start()
        flights.append(small)
    for t in reversed(range(plan.stages)):
        count = n_dp >> (t + 1)
        for j in range(n_opt):
            q = plan.peer(n_opt - j)
            if t == plan.stages - 1:
                if j > 0:
                    hops[j - 1].wait_recv()
            else:
                pending[j].wait_recv()
            where = out_ref.at[q, :, pl.ds(plan.base[t + 1], count)]
            copy = plan.to_partner(t, where, where, gs.at[t, j], gr.at[t, j])
            copy.start()
            if j == 0:
                fresh = []
            fresh.append(copy)
        pending = fresh
        flights.append(fresh)
    for copy in pending:
        copy.wait_recv()
    for copy in hops:
        copy.wait_send()
    for entry in flights:
        if isinstance(entry, list):
            for copy in entry:
                copy.wait_send()
        else:
            entry.wait()


def gather_weights(packed, small, n_dp, n_opt):
    groups, _, rows, width = packed.shape
    stages = n_dp.bit_length() - 1
    dma = pltpu.SemaphoreType.DMA
    return pl.pallas_call(
        functools.partial(gather_weights_kernel, n_dp, n_opt),
        out_shape=(
            jax.ShapeDtypeStruct((n_opt,) + packed.shape, packed.dtype),
            jax.ShapeDtypeStruct((n_opt,) + small.shape, small.dtype),
        ),
        in_specs=[pl.BlockSpec(memory_space=pltpu.VMEM)] * 2,
        out_specs=[pl.BlockSpec(memory_space=pltpu.VMEM)] * 2,
        scratch_shapes=[
            dma((n_opt,)), dma((n_opt,)), dma((n_opt,)), dma((n_opt,)),
            dma((stages, n_opt)), dma((stages, n_opt)),
        ],
        compiler_params=pltpu.CompilerParams(
            collective_id=0, has_side_effects=True, vmem_limit_bytes=48 * 2**20
        ),
        name="gather_weights",
    )(packed, small)


def reduce_kernel(n_dp, n_opt, grad_scale, g_ref, v_ref, m_ref, out_ref, vout_ref, *rest):
    plan = Plan(n_dp, n_opt)
    me, cid = plan.me, plan.chunk
    stages = plan.stages
    got = rest[:stages]
    acc = rest[stages : 2 * stages]
    zgot, mo, vgot, vacc, vz, ss, sr, zs, zr, ms, mr, gs, gr, vs, vr, us, ur = rest[2 * stages :]
    plan.barrier()
    sends = []

    def launch(t, j):
        half = n_dp >> (t + 1)
        q = plan.peer(j + 1)
        other = (1 - plan.bit[t]) * half
        src = (g_ref if t == 0 else acc[t - 1]).at[q, :, pl.ds(other, half)]
        copy = plan.to_partner(t, src, got[t].at[j], ss.at[t, j], sr.at[t, j])
        copy.start()
        return copy

    def launch_small(t):
        copy = plan.to_partner(
            t, v_ref if t == 0 else vacc.at[t - 1], vgot.at[t], vs.at[t], vr.at[t]
        )
        copy.start()
        return copy

    vcopy = launch_small(0)
    current = [launch(0, j) for j in range(n_opt)]
    zcopies = []
    vz_copies = []
    for t in range(stages):
        half = n_dp >> (t + 1)
        following = []
        for j in range(n_opt):
            q = plan.peer(j + 1)
            current[j].wait_recv()
            sends.append(current[j])
            source = g_ref if t == 0 else acc[t - 1]
            mine = plan.bit[t] * half
            kept = source[q, :, pl.ds(mine, half)].astype(F32)
            acc[t][q] = (kept + got[t][j].astype(F32)).astype(BF16)
            if t + 1 < stages:
                following.append(launch(t + 1, j))
            elif j < n_opt - 1:
                copy = plan.to_peer(j + 1, acc[t].at[q, :, 0], zgot.at[j], zs.at[j], zr.at[j])
                copy.start()
                zcopies.append(copy)
        current = following
        vcopy.wait_recv()
        sends.append(vcopy)
        vacc[t] = (v_ref[...] if t == 0 else vacc[t - 1]) + vgot[t]
        if t + 1 < stages:
            vcopy = launch_small(t + 1)
        else:
            for j in range(n_opt - 1):
                copy = plan.to_peer(
                    j + 1, vacc.at[t, plan.peer(j + 1)], vz.at[j], us.at[j], ur.at[j]
                )
                copy.start()
                vz_copies.append(copy)
    total = acc[stages - 1][me, :, 0].astype(F32)
    for j in range(n_opt - 1):
        zcopies[j].wait_recv()
        total = total + zgot[j].astype(F32)
    out_ref[0:3, cid] = total.astype(BF16)
    mo[...] = (MOMENTUM_DECAY * m_ref[:, cid] + total * grad_scale).astype(BF16)
    mcopies = []
    for j in range(1, n_opt):
        group = jnp.maximum(plan.peer(j) - 1, 0)
        copy = plan.to_peer(j, mo.at[group], out_ref.at[3 + me, cid], ms.at[j], mr.at[j])
        copy.start()
        mcopies.append(copy)
    out_ref[3 + me, cid] = mo[jnp.maximum(me - 1, 0)]
    vtotal = vacc[stages - 1, me]
    for j in range(n_opt - 1):
        vz_copies[j].wait_recv()
        vtotal = vtotal + vz[j]
    vout_ref[...] = vtotal
    for copy in mcopies:
        copy.wait_recv()
    for t in reversed(range(stages)):
        where = out_ref.at[:, pl.ds(plan.base[t + 1], n_dp >> (t + 1))]
        copy = plan.to_partner(t, where, where, gs.at[t], gr.at[t])
        copy.start()
        copy.wait_recv()
        sends.append(copy)
    for copy in sends + zcopies + vz_copies + mcopies:
        copy.wait_send()


def reduce_grads(packed, small, moms, grad_scale, n_dp, n_opt):
    _, groups, _, rows, width = packed.shape
    stages = n_dp.bit_length() - 1
    dma = pltpu.SemaphoreType.DMA
    halves = [
        pltpu.VMEM((n_opt, groups, n_dp >> (t + 1), rows, width), BF16) for t in range(stages)
    ]
    return pl.pallas_call(
        functools.partial(reduce_kernel, n_dp, n_opt, grad_scale),
        out_shape=(
            jax.ShapeDtypeStruct((groups + n_opt, n_dp, rows, width), BF16),
            jax.ShapeDtypeStruct(small.shape[1:], F32),
        ),
        in_specs=[pl.BlockSpec(memory_space=pltpu.VMEM)] * 3,
        out_specs=[pl.BlockSpec(memory_space=pltpu.VMEM)] * 2,
        scratch_shapes=halves
        + halves
        + [
            pltpu.VMEM((n_opt - 1, groups, rows, width), BF16),
            pltpu.VMEM((groups, rows, width), BF16),
            pltpu.VMEM((stages,) + small.shape, F32),
            pltpu.VMEM((stages,) + small.shape, F32),
            pltpu.VMEM((n_opt - 1,) + small.shape[1:], F32),
            dma((stages, n_opt)), dma((stages, n_opt)),
            dma((n_opt,)), dma((n_opt,)), dma((n_opt,)), dma((n_opt,)),
            dma((stages,)), dma((stages,)), dma((stages,)), dma((stages,)),
            dma((n_opt,)), dma((n_opt,)),
        ],
        compiler_params=pltpu.CompilerParams(
            collective_id=1, has_side_effects=True, vmem_limit_bytes=56 * 2**20
        ),
        name="reduce_grads",
    )(packed, small, moms)


def spread_kernel(n_dp, n_opt, first_chunks, o_ref, out_ref, zgot, zs, zr, gs, gr):
    plan = Plan(n_dp, n_opt)
    me, cid = plan.me, plan.chunk
    zgot[me] = o_ref[me, cid]
    plan.barrier()
    copies = []
    for j in range(1, n_opt):
        copy = plan.to_peer(j, o_ref.at[plan.peer(j), cid], zgot.at[me], zs.at[j], zr.at[j])
        copy.start()
        copies.append(copy)
    for copy in copies:
        copy.wait_recv()
    late = lax.div(cid, jnp.int32(first_chunks))
    out_ref[0, cid] = zgot[jnp.minimum(late, 1)]
    out_ref[1, cid] = zgot[2]
    out_ref[2, cid] = zgot[3]
    for t in reversed(range(plan.stages)):
        where = out_ref.at[:, pl.ds(plan.base[t + 1], n_dp >> (t + 1))]
        copy = plan.to_partner(t, where, where, gs.at[t], gr.at[t])
        copy.start()
        copy.wait_recv()
        copies.append(copy)
    for copy in copies:
        copy.wait_send()


def spread_updates(ortho, first_chunks, n_dp, n_opt):
    _, _, rows, width = ortho.shape
    stages = n_dp.bit_length() - 1
    dma = pltpu.SemaphoreType.DMA
    return pl.pallas_call(
        functools.partial(spread_kernel, n_dp, n_opt, first_chunks),
        out_shape=jax.ShapeDtypeStruct((3, n_dp, rows, width), BF16),
        in_specs=[pl.BlockSpec(memory_space=pltpu.VMEM)],
        out_specs=pl.BlockSpec(memory_space=pltpu.VMEM),
        scratch_shapes=[
            pltpu.VMEM((n_opt, rows, width), BF16),
            dma((n_opt,)), dma((n_opt,)), dma((stages,)), dma((stages,)),
        ],
        compiler_params=pltpu.CompilerParams(
            collective_id=2, has_side_effects=True, vmem_limit_bytes=48 * 2**20
        ),
        name="spread_updates",
    )(ortho)


def pair(values):
    high = values.astype(BF16)
    return high, (values - high.astype(F32)).astype(BF16)


def dot_rows(left, right):
    return lax.dot_general(left, right, (((1,), (1,)), ((), ())), preferred_element_type=F32)


def dot_plain(left, right):
    return lax.dot_general(left, right, (((1,), (0,)), ((), ())), preferred_element_type=F32)


def newton_kernel(n_opt, m_ref, out_ref, y_ref):
    rank = lax.axis_index("opt")
    _, width, _ = m_ref.shape
    part = width // n_opt

    @pl.when(rank < 3)
    def _():
        for q in range(n_opt):
            for b in range(4):
                is_proj = b == 3
                keep = (rank == 2) | ((rank == 1) if is_proj else (rank == 0))
                block = m_ref[q, b * part : (b + 1) * part, :].astype(F32)
                y_ref[q * part : (q + 1) * part, b * width : (b + 1) * width] = (
                    block * keep.astype(F32)
                )

    @pl.when(rank == 3)
    def _():
        for q in range(n_opt):
            y_ref[:, q * width : (q + 1) * width] = m_ref[q].astype(F32).T

    start = y_ref[...]
    norm = jnp.sqrt(jnp.sum(jnp.sum(start * start, 1, keepdims=True), 0, keepdims=True)) + 1e-07
    y_ref[...] = start / norm

    def sweep(_, carry):
        ortho = y_ref[...]
        high, low = pair(ortho)
        cross = dot_rows(high, low)
        gram = dot_rows(high, high) + (cross + cross.T)
        gram_high, gram_low = pair(gram)
        twist = dot_plain(gram_high, gram_low)
        square = dot_plain(gram_high, gram_high) + (twist + twist.T)
        poly = COEF_SECOND * gram + COEF_THIRD * square
        poly_high, poly_low = pair(poly)
        y_ref[...] = COEF_FIRST * ortho + (
            dot_plain(poly_high, high) + (dot_plain(poly_high, low) + dot_plain(poly_low, high))
        )
        return carry

    lax.fori_loop(0, NS_ITERS, sweep, 0)
    wide = math.sqrt(n_opt * width)
    middle = math.sqrt(3 * width)
    factor = MATRIX_FACTOR * jnp.where(
        rank == 0, middle, jnp.where(rank == 1, math.sqrt(width), wide)
    ).astype(F32)

    @pl.when(rank < 3)
    def _():
        for q in range(n_opt):
            for b in range(4):
                block = y_ref[q * part : (q + 1) * part, b * width : (b + 1) * width]
                out_ref[q, b * part : (b + 1) * part, :] = (block * factor).astype(BF16)

    @pl.when(rank == 3)
    def _():
        for q in range(n_opt):
            out_ref[q] = (y_ref[:, q * width : (q + 1) * width].T * factor).astype(BF16)


def newton_owned(mats):
    n_opt, width, _ = mats.shape
    return pl.pallas_call(
        functools.partial(newton_kernel, n_opt),
        out_shape=jax.ShapeDtypeStruct(mats.shape, BF16),
        in_specs=[pl.BlockSpec(memory_space=pltpu.VMEM)],
        out_specs=pl.BlockSpec(memory_space=pltpu.VMEM),
        scratch_shapes=[pltpu.VMEM((width, n_opt * width), F32)],
        compiler_params=pltpu.CompilerParams(vmem_limit_bytes=48 * 2**20),
        name="newton_owned",
    )(mats)


def stack_blocks(matrix, width):
    return jnp.concatenate(
        [matrix[:, i : i + width] for i in range(0, matrix.shape[1], width)], 0
    )


def unstack_blocks(stacked, rows):
    return jnp.concatenate(
        [stacked[i : i + rows] for i in range(0, stacked.shape[0], rows)], 1
    )


def pack_rows(qkv, proj, fc1, fc2):
    width = proj.shape[1]
    return jnp.stack(
        [
            jnp.concatenate([stack_blocks(qkv, width), proj], 0),
            stack_blocks(fc1, width),
            fc2,
        ]
    )


def unpack_rows(packed, part):
    both = packed[0]
    return (
        unstack_blocks(both[: 3 * part], part),
        both[3 * part :],
        unstack_blocks(packed[1], part),
        packed[2],
    )


def dot_cols(left, right):
    return lax.dot_general(left, right, (((0,), (0,)), ((), ())), preferred_element_type=F32)


def norm_rows(values):
    row_mean = jnp.mean(values, -1, keepdims=True)
    centered = values - row_mean
    inv_std = lax.rsqrt(jnp.mean(centered * centered, -1, keepdims=True) + NORM_EPSILON)
    return (centered * inv_std, inv_std)


def norm_back(grad_norm, normed, inv_std):
    return inv_std * (
        grad_norm
        - jnp.mean(grad_norm, -1, keepdims=True)
        - normed * jnp.mean(grad_norm * normed, -1, keepdims=True)
    )


def layer_kernel(
    seq_len, seq_pad, small_count,
    x_ref, c_ref, w_ref, v_ref, out_ref, gx_ref, g_ref, gv_ref,
    rows_s, cot_s, wide_s, qkv_s, probs_s, att_s, datt_s, dqkv_s, mid_s, gmid_s,
):
    n_img = x_ref.shape[0]
    n_opt, _, width, _ = w_ref.shape
    part = width // n_opt
    scale = HEAD_DIM ** (-0.5)

    def vec(r):
        return v_ref[r // small_count, r % small_count : r % small_count + 1, :]

    def put_vec(r, row):
        gv_ref[r // small_count, r % small_count : r % small_count + 1, :] = row

    def col_sum(values):
        return jnp.sum(values, 0, keepdims=True)

    rows_s[...] = jnp.zeros_like(rows_s)
    cot_s[...] = jnp.zeros_like(cot_s)
    gv_ref[...] = jnp.zeros_like(gv_ref)
    for i in range(n_img):
        rows_s[i * seq_pad : i * seq_pad + seq_len, :] = x_ref[i].astype(F32)
        cot_s[i * seq_pad : i * seq_pad + seq_len, :] = c_ref[i].astype(F32)
    for g in range(2):
        for b in range(4):
            for q in range(n_opt):
                wide_s[g, b, q * part : (q + 1) * part, :] = w_ref[
                    q, g, b * part : (b + 1) * part, :
                ]

    normed_one, inv_one = norm_rows(rows_s[...])
    act_one = (normed_one * vec(0) + vec(1)).astype(BF16)
    qkv_s[0] = (dot_plain(act_one, wide_s[0, 0]) + vec(2)).astype(BF16)
    qkv_s[1] = dot_plain(act_one, wide_s[0, 1]).astype(BF16)
    qkv_s[2] = (dot_plain(act_one, wide_s[0, 2]) + vec(3)).astype(BF16)

    lanes = 2 * HEAD_DIM
    pairs = width // lanes
    left_lane = lax.broadcasted_iota(jnp.int32, (seq_pad, lanes), 1) < HEAD_DIM
    real_key = lax.broadcasted_iota(jnp.int32, (seq_pad, seq_pad), 1) < seq_len

    def only(values, side):
        keep = left_lane if side == 0 else jnp.logical_not(left_lane)
        return jnp.where(keep, values.astype(F32), 0.0).astype(BF16)

    def join(sides):
        return jnp.where(left_lane, sides[0], sides[1])

    def forward(i, carry):
        at = pl.ds(pl.multiple_of(i * seq_pad, 16), seq_pad)
        for p in range(pairs):
            col = slice(p * lanes, (p + 1) * lanes)
            queries, keys, values = qkv_s[0, at, col], qkv_s[1, at, col], qkv_s[2, at, col]
            sides = []
            for side in range(2):
                scores = dot_rows(only(queries, side), keys) * scale
                scores = jnp.where(real_key, scores, -1e30)
                top = jnp.max(scores, -1, keepdims=True)
                weight = jnp.exp(scores - top)
                probs = weight / jnp.sum(weight, -1, keepdims=True)
                probs_s[i, 2 * p + side] = probs
                sides.append(dot_plain(probs.astype(BF16), values))
            att_s[at, col] = join(sides).astype(BF16)
        return carry

    lax.fori_loop(0, n_img, forward, 0)
    mid_s[...] = rows_s[...] + dot_plain(att_s[...], wide_s[0, 3]) + vec(4)
    normed_two, inv_two = norm_rows(mid_s[...])
    act_two = (normed_two * vec(5) + vec(6)).astype(BF16)
    cot_low = cot_s[...].astype(BF16)
    result = mid_s[...] + vec(7)
    grad_act_two = jnp.zeros_like(result)
    for b in range(4):
        hidden_pre = dot_plain(act_two, wide_s[1, b]) + vec(8 + b)
        normal_cdf = 0.5 * (1.0 + lax.erf(hidden_pre * ROOT_HALF))
        hidden = (hidden_pre * normal_cdf).astype(BF16)
        result = result + dot_plain(hidden, w_ref[b, 2])
        g_ref[b, 2] = dot_cols(hidden, cot_low).astype(BF16)
        slope = normal_cdf + hidden_pre * jnp.exp(-0.5 * hidden_pre * hidden_pre) * INV_ROOT_TAU
        grad_pre = dot_rows(cot_low, w_ref[b, 2]) * slope
        put_vec(8 + b, col_sum(grad_pre))
        pre_low = grad_pre.astype(BF16)
        grad = dot_cols(act_two, pre_low).astype(BF16)
        for q in range(n_opt):
            g_ref[q, 1, b * part : (b + 1) * part, :] = grad[q * part : (q + 1) * part]
        grad_act_two = grad_act_two + dot_rows(pre_low, wide_s[1, b])
    mid_s[...] = result
    for i in range(n_img):
        out_ref[i] = mid_s[i * seq_pad : i * seq_pad + seq_len, :].astype(BF16)
    put_vec(7, col_sum(cot_s[...]))
    put_vec(5, col_sum(grad_act_two * normed_two))
    put_vec(6, col_sum(grad_act_two))
    grad_middle = cot_s[...] + norm_back(grad_act_two * vec(5), normed_two, inv_two)
    gmid_s[...] = grad_middle
    put_vec(4, col_sum(grad_middle))
    middle_low = grad_middle.astype(BF16)
    grad = dot_cols(att_s[...], middle_low).astype(BF16)
    for q in range(n_opt):
        g_ref[q, 0, 3 * part : 4 * part, :] = grad[q * part : (q + 1) * part]
    datt_s[...] = dot_rows(middle_low, wide_s[0, 3]).astype(BF16)

    def backward(i, carry):
        at = pl.ds(pl.multiple_of(i * seq_pad, 16), seq_pad)
        for p in range(pairs):
            col = slice(p * lanes, (p + 1) * lanes)
            queries, keys, values = qkv_s[0, at, col], qkv_s[1, at, col], qkv_s[2, at, col]
            datt = datt_s[at, col]
            grads = ([], [], [])
            for side in range(2):
                probs = probs_s[i, 2 * p + side]
                grads[2].append(dot_cols(probs.astype(BF16), datt))
                grad_probs = dot_rows(only(datt, side), values)
                row_dot = jnp.sum(probs * grad_probs, -1, keepdims=True)
                grad_scores = (probs * (grad_probs - row_dot) * scale).astype(BF16)
                grads[0].append(dot_plain(grad_scores, keys))
                grads[1].append(dot_cols(grad_scores, queries))
            for k in range(3):
                dqkv_s[k, at, col] = join(grads[k])
        return carry

    lax.fori_loop(0, n_img, backward, 0)
    put_vec(2, col_sum(dqkv_s[0]))
    put_vec(3, col_sum(dqkv_s[2]))
    normed_one, inv_one = norm_rows(rows_s[...])
    act_one = (normed_one * vec(0) + vec(1)).astype(BF16)
    grad_act_one = jnp.zeros_like(normed_one)
    for k in range(3):
        low = dqkv_s[k].astype(BF16)
        grad = dot_cols(act_one, low).astype(BF16)
        for q in range(n_opt):
            g_ref[q, 0, k * part : (k + 1) * part, :] = grad[q * part : (q + 1) * part]
        grad_act_one = grad_act_one + dot_rows(low, wide_s[0, k])
    put_vec(0, col_sum(grad_act_one * normed_one))
    put_vec(1, col_sum(grad_act_one))
    mid_s[...] = gmid_s[...] + norm_back(grad_act_one * vec(0), normed_one, inv_one)
    for i in range(n_img):
        gx_ref[i] = mid_s[i * seq_pad : i * seq_pad + seq_len, :].astype(BF16)


def layer_step(tokens, cotangent, weights, small, small_count):
    n_img, seq_len, width = tokens.shape
    seq_pad = seq_len + -seq_len % 16
    total = n_img * seq_pad
    heads = width // HEAD_DIM
    vmem = pl.BlockSpec(memory_space=pltpu.VMEM)
    return pl.pallas_call(
        functools.partial(layer_kernel, seq_len, seq_pad, small_count),
        out_shape=(
            jax.ShapeDtypeStruct(tokens.shape, BF16),
            jax.ShapeDtypeStruct(tokens.shape, BF16),
            jax.ShapeDtypeStruct(weights.shape, BF16),
            jax.ShapeDtypeStruct(small.shape, F32),
        ),
        in_specs=[vmem] * 4,
        out_specs=[vmem] * 4,
        scratch_shapes=[
            pltpu.VMEM((total, width), F32),
            pltpu.VMEM((total, width), F32),
            pltpu.VMEM((2, 4, width, width), BF16),
            pltpu.VMEM((3, total, width), BF16),
            pltpu.VMEM((n_img, heads, seq_pad, seq_pad), F32),
            pltpu.VMEM((total, width), BF16),
            pltpu.VMEM((total, width), BF16),
            pltpu.VMEM((3, total, width), F32),
            pltpu.VMEM((total, width), F32),
            pltpu.VMEM((total, width), F32),
        ],
        compiler_params=pltpu.CompilerParams(vmem_limit_bytes=56 * 2**20),
        name="layer_step",
    )(tokens, cotangent, weights, small)


def body(
    tokens,
    cotangent,
    w_qkv,
    w_proj,
    w_fc1,
    w_fc2,
    vectors,
    mom_qkv,
    mom_proj,
    mom_fc1,
    mom_fc2,
    mom_vectors,
):
    n_dp, n_opt = lax.axis_size("dp"), lax.axis_size("opt")
    part, width = w_proj.shape
    rows = width // n_dp
    small_count = vectors.shape[0]
    pad = -small_count % 8

    def cut(packed):
        return packed.reshape(packed.shape[:-2] + (n_dp, rows, width))

    def join(packed):
        return packed.reshape(packed.shape[:-3] + (width, width))

    weights_mine = cut(pack_rows(*[w.astype(BF16) for w in (w_qkv, w_proj, w_fc1, w_fc2)]))
    small_mine = jnp.pad(vectors.astype(BF16).astype(F32), ((0, pad), (0, 0)))
    all_weights, all_small = gather_weights(weights_mine, small_mine, n_dp, n_opt)
    all_weights = join(all_weights)
    outputs, grad_tokens, packed, small = layer_step(
        tokens, cotangent, all_weights, all_small, small_count
    )
    packed = cut(packed)
    token_total = tokens.shape[0] * tokens.shape[1] * n_dp * n_opt
    grad_scale = 1.0 / math.sqrt(token_total)
    moms = cut(pack_rows(mom_qkv, mom_proj, mom_fc1, mom_fc2))
    summed, small_sum = reduce_grads(packed, small, moms, grad_scale, n_dp, n_opt)
    summed = join(summed)
    shares = tuple(x.astype(F32) for x in unpack_rows(summed[:3], part)) + (
        small_sum[:small_count],
    )
    old_moms = (mom_qkv, mom_proj, mom_fc1, mom_fc2, mom_vectors)
    new_moms = tuple(
        (
            MOMENTUM_DECAY * old_state + share_part * grad_scale
            for old_state, share_part in zip(old_moms, shares)
        )
    )
    vector_mom = new_moms[4]
    new_vectors = vectors - VECTOR_RATE * vector_mom * lax.rsqrt(
        jnp.mean(vector_mom * vector_mom, -1, keepdims=True) + NORM_EPSILON
    )
    ortho = newton_owned(summed[3:])
    updates = join(spread_updates(cut(ortho), 3 * part // rows, n_dp, n_opt))
    new_mats = tuple(
        (
            weight_now - update_part.astype(F32)
            for weight_now, update_part in zip(
                (w_qkv, w_proj, w_fc1, w_fc2), unpack_rows(updates, part)
            )
        )
    )
    return (outputs, grad_tokens) + shares + new_mats + (new_vectors,) + new_moms


def solution(mesh):
    return jax.shard_map(
        body,
        mesh=mesh,
        in_specs=(
            P(("dp", "opt"), None, None),
            P(("dp", "opt"), None, None),
            P("opt", None),
            P("opt", None),
            P("opt", None),
            P("opt", None),
            P("opt", None),
            P("opt", None),
            P("opt", None),
            P("opt", None),
            P("opt", None),
            P("opt", None),
        ),
        out_specs=(
            P(("dp", "opt"), None, None),
            P(("dp", "opt"), None, None),
            P("opt", None),
            P("opt", None),
            P("opt", None),
            P("opt", None),
            P("opt", None),
            P("opt", None),
            P("opt", None),
            P("opt", None),
            P("opt", None),
            P("opt", None),
            P("opt", None),
            P("opt", None),
            P("opt", None),
            P("opt", None),
            P("opt", None),
        ),
        check_vma=False,
    )
```

```python
import functools
import math

import jax
import jax.numpy as jnp
from jax import lax
from jax.experimental import pallas as pl
from jax.experimental.pallas import tpu as pltpu
from jax.sharding import PartitionSpec as P

HEAD_DIM = 64
NS_ITERS = 5


NORM_EPSILON = 1e-06
MOMENTUM_DECAY = 0.9
VECTOR_RATE = 0.2
MATRIX_FACTOR = 0.04
COEF_FIRST = 3.4445
COEF_SECOND = -4.775
COEF_THIRD = 2.0315
ROOT_HALF = 0.7071067811865476
INV_ROOT_TAU = 0.3989422804014327

MESH = pl.DeviceIdType.MESH
BF16 = jnp.bfloat16
F32 = jnp.float32


class Plan:
    def __init__(self, n_dp, n_opt):
        self.n_dp, self.n_opt = n_dp, n_opt
        self.me = lax.axis_index("opt")
        dp = lax.axis_index("dp")
        self.dp = dp
        self.stages = n_dp.bit_length() - 1
        bits = [lax.rem(lax.div(dp, jnp.int32(2**p)), jnp.int32(2)) for p in range(self.stages)]
        core = bits[0]
        self.bit, self.partner, self.base = [], [], [jnp.int32(0)]
        for t in range(self.stages):
            up = t
            down = 0 if t == 0 else self.stages - t
            bit = bits[up] + core * (bits[down] - bits[up]) if t else bits[0]
            weight = 2**up + core * (2**down - 2**up) if t else 1
            self.bit.append(bit)
            self.partner.append(dp + weight * (1 - 2 * bit))
            self.base.append(self.base[-1] + bit * (n_dp >> (t + 1)))
        self.chunk = self.base[-1]

    def peer(self, j):
        return lax.rem(self.me + j, jnp.int32(self.n_opt))

    def barrier(self):
        sem = pltpu.get_barrier_semaphore()
        for t in range(self.stages):
            pl.semaphore_signal(
                sem, inc=1, device_id=(self.partner[t], self.me), device_id_type=MESH
            )
        for j in range(1, self.n_opt):
            pl.semaphore_signal(
                sem, inc=1, device_id=(self.dp, self.peer(j)), device_id_type=MESH
            )
        pl.semaphore_wait(sem, self.stages + self.n_opt - 1)

    def to_partner(self, t, src, dst, send, recv):
        return pltpu.make_async_remote_copy(
            src_ref=src, dst_ref=dst, send_sem=send, recv_sem=recv,
            device_id=(self.partner[t], self.me), device_id_type=MESH,
        )

    def to_peer(self, j, src, dst, send, recv):
        return pltpu.make_async_remote_copy(
            src_ref=src, dst_ref=dst, send_sem=send, recv_sem=recv,
            device_id=(self.dp, self.peer(j)), device_id_type=MESH,
        )


def gather_weights_kernel(n_dp, n_opt, w_ref, v_ref, out_ref, vout_ref, zs, zr, vs, vr, gs, gr):
    plan = Plan(n_dp, n_opt)
    me, cid = plan.me, plan.chunk
    out_ref[me, :, cid] = w_ref[:, cid]
    vout_ref[me] = v_ref[...]
    plan.barrier()
    flights = []
    hops = []
    for j in range(1, n_opt):
        copy = plan.to_peer(
            j, w_ref.at[:, cid], out_ref.at[me, :, cid], zs.at[j], zr.at[j]
        )
        copy.start()
        hops.append(copy)
        small = plan.to_peer(j, v_ref, vout_ref.at[me], vs.at[j], vr.at[j])
        small.start()
        flights.append(small)
    for t in reversed(range(plan.stages)):
        count = n_dp >> (t + 1)
        for j in range(n_opt):
            q = plan.peer(n_opt - j)
            if t == plan.stages - 1:
                if j > 0:
                    hops[j - 1].wait_recv()
            else:
                pending[j].wait_recv()
            where = out_ref.at[q, :, pl.ds(plan.base[t + 1], count)]
            copy = plan.to_partner(t, where, where, gs.at[t, j], gr.at[t, j])
            copy.start()
            if j == 0:
                fresh = []
            fresh.append(copy)
        pending = fresh
        flights.append(fresh)
    for copy in pending:
        copy.wait_recv()
    for copy in hops:
        copy.wait_send()
    for entry in flights:
        if isinstance(entry, list):
            for copy in entry:
                copy.wait_send()
        else:
            entry.wait()


def gather_weights(packed, small, n_dp, n_opt):
    groups, _, rows, width = packed.shape
    stages = n_dp.bit_length() - 1
    dma = pltpu.SemaphoreType.DMA
    return pl.pallas_call(
        functools.partial(gather_weights_kernel, n_dp, n_opt),
        out_shape=(
            jax.ShapeDtypeStruct((n_opt,) + packed.shape, packed.dtype),
            jax.ShapeDtypeStruct((n_opt,) + small.shape, small.dtype),
        ),
        in_specs=[pl.BlockSpec(memory_space=pltpu.VMEM)] * 2,
        out_specs=[pl.BlockSpec(memory_space=pltpu.VMEM)] * 2,
        scratch_shapes=[
            dma((n_opt,)), dma((n_opt,)), dma((n_opt,)), dma((n_opt,)),
            dma((stages, n_opt)), dma((stages, n_opt)),
        ],
        compiler_params=pltpu.CompilerParams(
            collective_id=0, has_side_effects=True, vmem_limit_bytes=48 * 2**20
        ),
        name="gather_weights",
    )(packed, small)


def reduce_kernel(n_dp, n_opt, grad_scale, g_ref, v_ref, m_ref, out_ref, vout_ref, *rest):
    plan = Plan(n_dp, n_opt)
    me, cid = plan.me, plan.chunk
    stages = plan.stages
    got = rest[:stages]
    acc = rest[stages : 2 * stages]
    zgot, mo, vgot, vacc, vz, ss, sr, zs, zr, ms, mr, gs, gr, vs, vr, us, ur = rest[2 * stages :]
    plan.barrier()
    sends = []

    def launch(t, j):
        half = n_dp >> (t + 1)
        q = plan.peer(j + 1)
        other = (1 - plan.bit[t]) * half
        src = (g_ref if t == 0 else acc[t - 1]).at[q, :, pl.ds(other, half)]
        copy = plan.to_partner(t, src, got[t].at[j], ss.at[t, j], sr.at[t, j])
        copy.start()
        return copy

    def launch_small(t):
        copy = plan.to_partner(
            t, v_ref if t == 0 else vacc.at[t - 1], vgot.at[t], vs.at[t], vr.at[t]
        )
        copy.start()
        return copy

    vcopy = launch_small(0)
    current = [launch(0, j) for j in range(n_opt)]
    zcopies = []
    vz_copies = []
    for t in range(stages):
        half = n_dp >> (t + 1)
        following = []
        for j in range(n_opt):
            q = plan.peer(j + 1)
            current[j].wait_recv()
            sends.append(current[j])
            source = g_ref if t == 0 else acc[t - 1]
            mine = plan.bit[t] * half
            kept = source[q, :, pl.ds(mine, half)].astype(F32)
            acc[t][q] = (kept + got[t][j].astype(F32)).astype(BF16)
            if t + 1 < stages:
                following.append(launch(t + 1, j))
            elif j < n_opt - 1:
                copy = plan.to_peer(j + 1, acc[t].at[q, :, 0], zgot.at[j], zs.at[j], zr.at[j])
                copy.start()
                zcopies.append(copy)
        current = following
        vcopy.wait_recv()
        sends.append(vcopy)
        vacc[t] = (v_ref[...] if t == 0 else vacc[t - 1]) + vgot[t]
        if t + 1 < stages:
            vcopy = launch_small(t + 1)
        else:
            for j in range(n_opt - 1):
                copy = plan.to_peer(
                    j + 1, vacc.at[t, plan.peer(j + 1)], vz.at[j], us.at[j], ur.at[j]
                )
                copy.start()
                vz_copies.append(copy)
    total = acc[stages - 1][me, :, 0].astype(F32)
    for j in range(n_opt - 1):
        zcopies[j].wait_recv()
        total = total + zgot[j].astype(F32)
    out_ref[0:3, cid] = total.astype(BF16)
    pieces = ((0, 3), (3, n_opt // 2), (3 + n_opt // 2, n_opt - n_opt // 2))

    def spread(t, k):
        first, count = pieces[k]
        where = out_ref.at[pl.ds(first, count), pl.ds(plan.base[t + 1], n_dp >> (t + 1))]
        copy = plan.to_partner(t, where, where, gs.at[t, k], gr.at[t, k])
        copy.start()
        sends.append(copy)
        return copy

    pending = [spread(stages - 1, 0)]
    mo[...] = (MOMENTUM_DECAY * m_ref[:, cid] + total * grad_scale).astype(BF16)
    mcopies = []
    for j in range(1, n_opt):
        group = jnp.maximum(plan.peer(j) - 1, 0)
        copy = plan.to_peer(j, mo.at[group], out_ref.at[3 + me, cid], ms.at[j], mr.at[j])
        copy.start()
        mcopies.append(copy)
    out_ref[3 + me, cid] = mo[jnp.maximum(me - 1, 0)]
    vtotal = vacc[stages - 1, me]
    for j in range(n_opt - 1):
        vz_copies[j].wait_recv()
        vtotal = vtotal + vz[j]
    vout_ref[...] = vtotal
    for copy in mcopies:
        copy.wait_recv()
    for k in range(1, len(pieces)):
        pending.append(spread(stages - 1, k))
    for t in reversed(range(stages - 1)):
        for k in range(len(pieces)):
            pending[k].wait_recv()
            pending[k] = spread(t, k)
    for copy in pending:
        copy.wait_recv()
    for copy in sends + zcopies + vz_copies + mcopies:
        copy.wait_send()


def reduce_grads(packed, small, moms, grad_scale, n_dp, n_opt):
    _, groups, _, rows, width = packed.shape
    stages = n_dp.bit_length() - 1
    dma = pltpu.SemaphoreType.DMA
    halves = [
        pltpu.VMEM((n_opt, groups, n_dp >> (t + 1), rows, width), BF16) for t in range(stages)
    ]
    return pl.pallas_call(
        functools.partial(reduce_kernel, n_dp, n_opt, grad_scale),
        out_shape=(
            jax.ShapeDtypeStruct((groups + n_opt, n_dp, rows, width), BF16),
            jax.ShapeDtypeStruct(small.shape[1:], F32),
        ),
        in_specs=[pl.BlockSpec(memory_space=pltpu.VMEM)] * 3,
        out_specs=[pl.BlockSpec(memory_space=pltpu.VMEM)] * 2,
        scratch_shapes=halves
        + halves
        + [
            pltpu.VMEM((n_opt - 1, groups, rows, width), BF16),
            pltpu.VMEM((groups, rows, width), BF16),
            pltpu.VMEM((stages,) + small.shape, F32),
            pltpu.VMEM((stages,) + small.shape, F32),
            pltpu.VMEM((n_opt - 1,) + small.shape[1:], F32),
            dma((stages, n_opt)), dma((stages, n_opt)),
            dma((n_opt,)), dma((n_opt,)), dma((n_opt,)), dma((n_opt,)),
            dma((stages, 3)), dma((stages, 3)), dma((stages,)), dma((stages,)),
            dma((n_opt,)), dma((n_opt,)),
        ],
        compiler_params=pltpu.CompilerParams(
            collective_id=1, has_side_effects=True, vmem_limit_bytes=56 * 2**20
        ),
        name="reduce_grads",
    )(packed, small, moms)


def spread_kernel(n_dp, n_opt, first_chunks, o_ref, out_ref, zgot, zs, zr, gs, gr):
    plan = Plan(n_dp, n_opt)
    me, cid = plan.me, plan.chunk
    zgot[me] = o_ref[me, cid]
    plan.barrier()
    copies = []
    for j in range(1, n_opt):
        copy = plan.to_peer(j, o_ref.at[plan.peer(j), cid], zgot.at[me], zs.at[j], zr.at[j])
        copy.start()
        copies.append(copy)
    for copy in copies:
        copy.wait_recv()
    late = lax.div(cid, jnp.int32(first_chunks))
    out_ref[0, cid] = zgot[jnp.minimum(late, 1)]
    out_ref[1, cid] = zgot[2]
    out_ref[2, cid] = zgot[3]
    pending = [None] * 3
    for t in reversed(range(plan.stages)):
        for k in range(3):
            if pending[k] is not None:
                pending[k].wait_recv()
            where = out_ref.at[k, pl.ds(plan.base[t + 1], n_dp >> (t + 1))]
            pending[k] = plan.to_partner(t, where, where, gs.at[t, k], gr.at[t, k])
            pending[k].start()
            copies.append(pending[k])
    for copy in pending:
        copy.wait_recv()
    for copy in copies:
        copy.wait_send()


def spread_updates(ortho, first_chunks, n_dp, n_opt):
    _, _, rows, width = ortho.shape
    stages = n_dp.bit_length() - 1
    dma = pltpu.SemaphoreType.DMA
    return pl.pallas_call(
        functools.partial(spread_kernel, n_dp, n_opt, first_chunks),
        out_shape=jax.ShapeDtypeStruct((3, n_dp, rows, width), BF16),
        in_specs=[pl.BlockSpec(memory_space=pltpu.VMEM)],
        out_specs=pl.BlockSpec(memory_space=pltpu.VMEM),
        scratch_shapes=[
            pltpu.VMEM((n_opt, rows, width), BF16),
            dma((n_opt,)), dma((n_opt,)), dma((stages, 3)), dma((stages, 3)),
        ],
        compiler_params=pltpu.CompilerParams(
            collective_id=2, has_side_effects=True, vmem_limit_bytes=48 * 2**20
        ),
        name="spread_updates",
    )(ortho)


def pair(values):
    high = values.astype(BF16)
    return high, (values - high.astype(F32)).astype(BF16)


def dot_rows(left, right):
    return lax.dot_general(left, right, (((1,), (1,)), ((), ())), preferred_element_type=F32)


def dot_plain(left, right):
    return lax.dot_general(left, right, (((1,), (0,)), ((), ())), preferred_element_type=F32)


def newton_kernel(n_opt, m_ref, out_ref, y_ref):
    rank = lax.axis_index("opt")
    _, width, _ = m_ref.shape
    part = width // n_opt

    @pl.when(rank < 3)
    def _():
        for q in range(n_opt):
            for b in range(4):
                is_proj = b == 3
                keep = (rank == 2) | ((rank == 1) if is_proj else (rank == 0))
                block = m_ref[q, b * part : (b + 1) * part, :].astype(F32)
                y_ref[q * part : (q + 1) * part, b * width : (b + 1) * width] = (
                    block * keep.astype(F32)
                )

    @pl.when(rank == 3)
    def _():
        for q in range(n_opt):
            y_ref[:, q * width : (q + 1) * width] = m_ref[q].astype(F32).T

    start = y_ref[...]
    norm = jnp.sqrt(jnp.sum(jnp.sum(start * start, 1, keepdims=True), 0, keepdims=True)) + 1e-07
    y_ref[...] = start / norm

    def sweep(_, carry):
        ortho = y_ref[...]
        high, low = pair(ortho)
        cross = dot_rows(high, low)
        gram = dot_rows(high, high) + (cross + cross.T)
        gram_high, gram_low = pair(gram)
        twist = dot_plain(gram_high, gram_low)
        square = dot_plain(gram_high, gram_high) + (twist + twist.T)
        poly = COEF_SECOND * gram + COEF_THIRD * square
        poly_high, poly_low = pair(poly)
        y_ref[...] = COEF_FIRST * ortho + (
            dot_plain(poly_high, high) + (dot_plain(poly_high, low) + dot_plain(poly_low, high))
        )
        return carry

    lax.fori_loop(0, NS_ITERS, sweep, 0)
    wide = math.sqrt(n_opt * width)
    middle = math.sqrt(3 * width)
    factor = MATRIX_FACTOR * jnp.where(
        rank == 0, middle, jnp.where(rank == 1, math.sqrt(width), wide)
    ).astype(F32)

    @pl.when(rank < 3)
    def _():
        for q in range(n_opt):
            for b in range(4):
                block = y_ref[q * part : (q + 1) * part, b * width : (b + 1) * width]
                out_ref[q, b * part : (b + 1) * part, :] = (block * factor).astype(BF16)

    @pl.when(rank == 3)
    def _():
        for q in range(n_opt):
            out_ref[q] = (y_ref[:, q * width : (q + 1) * width].T * factor).astype(BF16)


def newton_owned(mats):
    n_opt, width, _ = mats.shape
    return pl.pallas_call(
        functools.partial(newton_kernel, n_opt),
        out_shape=jax.ShapeDtypeStruct(mats.shape, BF16),
        in_specs=[pl.BlockSpec(memory_space=pltpu.VMEM)],
        out_specs=pl.BlockSpec(memory_space=pltpu.VMEM),
        scratch_shapes=[pltpu.VMEM((width, n_opt * width), F32)],
        compiler_params=pltpu.CompilerParams(vmem_limit_bytes=48 * 2**20),
        name="newton_owned",
    )(mats)


def stack_blocks(matrix, width):
    return jnp.concatenate(
        [matrix[:, i : i + width] for i in range(0, matrix.shape[1], width)], 0
    )


def unstack_blocks(stacked, rows):
    return jnp.concatenate(
        [stacked[i : i + rows] for i in range(0, stacked.shape[0], rows)], 1
    )


def pack_rows(qkv, proj, fc1, fc2):
    width = proj.shape[1]
    return jnp.stack(
        [
            jnp.concatenate([stack_blocks(qkv, width), proj], 0),
            stack_blocks(fc1, width),
            fc2,
        ]
    )


def unpack_rows(packed, part):
    both = packed[0]
    return (
        unstack_blocks(both[: 3 * part], part),
        both[3 * part :],
        unstack_blocks(packed[1], part),
        packed[2],
    )


def dot_cols(left, right):
    return lax.dot_general(left, right, (((0,), (0,)), ((), ())), preferred_element_type=F32)


def norm_rows(values):
    row_mean = jnp.mean(values, -1, keepdims=True)
    centered = values - row_mean
    inv_std = lax.rsqrt(jnp.mean(centered * centered, -1, keepdims=True) + NORM_EPSILON)
    return (centered * inv_std, inv_std)


def norm_back(grad_norm, normed, inv_std):
    return inv_std * (
        grad_norm
        - jnp.mean(grad_norm, -1, keepdims=True)
        - normed * jnp.mean(grad_norm * normed, -1, keepdims=True)
    )


def layer_kernel(
    seq_len, seq_pad, small_count,
    x_ref, c_ref, w_ref, v_ref, out_ref, gx_ref, g_ref, gv_ref,
    rows_s, cot_s, wide_s, qkv_s, probs_s, att_s, datt_s, dqkv_s, mid_s, gmid_s,
):
    n_img = x_ref.shape[0]
    n_opt, _, width, _ = w_ref.shape
    part = width // n_opt
    scale = HEAD_DIM ** (-0.5)

    def vec(r):
        return v_ref[r // small_count, r % small_count : r % small_count + 1, :]

    def put_vec(r, row):
        gv_ref[r // small_count, r % small_count : r % small_count + 1, :] = row

    def col_sum(values):
        return jnp.sum(values, 0, keepdims=True)

    rows_s[...] = jnp.zeros_like(rows_s)
    cot_s[...] = jnp.zeros_like(cot_s)
    gv_ref[...] = jnp.zeros_like(gv_ref)
    for i in range(n_img):
        rows_s[i * seq_pad : i * seq_pad + seq_len, :] = x_ref[i].astype(F32)
        cot_s[i * seq_pad : i * seq_pad + seq_len, :] = c_ref[i].astype(F32)
    for g in range(2):
        for b in range(4):
            for q in range(n_opt):
                wide_s[g, b, q * part : (q + 1) * part, :] = w_ref[
                    q, g, b * part : (b + 1) * part, :
                ]

    normed_one, inv_one = norm_rows(rows_s[...])
    act_one = (normed_one * vec(0) + vec(1)).astype(BF16)
    qkv_s[0] = (dot_plain(act_one, wide_s[0, 0]) + vec(2)).astype(BF16)
    qkv_s[1] = dot_plain(act_one, wide_s[0, 1]).astype(BF16)
    qkv_s[2] = (dot_plain(act_one, wide_s[0, 2]) + vec(3)).astype(BF16)

    lanes = 2 * HEAD_DIM
    pairs = width // lanes
    left_lane = lax.broadcasted_iota(jnp.int32, (seq_pad, lanes), 1) < HEAD_DIM
    real_key = lax.broadcasted_iota(jnp.int32, (seq_pad, seq_pad), 1) < seq_len

    def only(values, side):
        keep = left_lane if side == 0 else jnp.logical_not(left_lane)
        return jnp.where(keep, values.astype(F32), 0.0).astype(BF16)

    def join(sides):
        return jnp.where(left_lane, sides[0], sides[1])

    def forward(i, carry):
        at = pl.ds(pl.multiple_of(i * seq_pad, 16), seq_pad)
        for p in range(pairs):
            col = slice(p * lanes, (p + 1) * lanes)
            queries, keys, values = qkv_s[0, at, col], qkv_s[1, at, col], qkv_s[2, at, col]
            sides = []
            for side in range(2):
                scores = dot_rows(only(queries, side), keys) * scale
                scores = jnp.where(real_key, scores, -1e30)
                top = jnp.max(scores, -1, keepdims=True)
                weight = jnp.exp(scores - top)
                probs = weight / jnp.sum(weight, -1, keepdims=True)
                probs_s[i, 2 * p + side] = probs
                sides.append(dot_plain(probs.astype(BF16), values))
            att_s[at, col] = join(sides).astype(BF16)
        return carry

    lax.fori_loop(0, n_img, forward, 0)
    mid_s[...] = rows_s[...] + dot_plain(att_s[...], wide_s[0, 3]) + vec(4)
    normed_two, inv_two = norm_rows(mid_s[...])
    act_two = (normed_two * vec(5) + vec(6)).astype(BF16)
    cot_low = cot_s[...].astype(BF16)
    result = mid_s[...] + vec(7)
    grad_act_two = jnp.zeros_like(result)
    for b in range(4):
        hidden_pre = dot_plain(act_two, wide_s[1, b]) + vec(8 + b)
        normal_cdf = 0.5 * (1.0 + lax.erf(hidden_pre * ROOT_HALF))
        hidden = (hidden_pre * normal_cdf).astype(BF16)
        result = result + dot_plain(hidden, w_ref[b, 2])
        g_ref[b, 2] = dot_cols(hidden, cot_low).astype(BF16)
        slope = normal_cdf + hidden_pre * jnp.exp(-0.5 * hidden_pre * hidden_pre) * INV_ROOT_TAU
        grad_pre = dot_rows(cot_low, w_ref[b, 2]) * slope
        put_vec(8 + b, col_sum(grad_pre))
        pre_low = grad_pre.astype(BF16)
        grad = dot_cols(act_two, pre_low).astype(BF16)
        for q in range(n_opt):
            g_ref[q, 1, b * part : (b + 1) * part, :] = grad[q * part : (q + 1) * part]
        grad_act_two = grad_act_two + dot_rows(pre_low, wide_s[1, b])
    mid_s[...] = result
    for i in range(n_img):
        out_ref[i] = mid_s[i * seq_pad : i * seq_pad + seq_len, :].astype(BF16)
    put_vec(7, col_sum(cot_s[...]))
    put_vec(5, col_sum(grad_act_two * normed_two))
    put_vec(6, col_sum(grad_act_two))
    grad_middle = cot_s[...] + norm_back(grad_act_two * vec(5), normed_two, inv_two)
    gmid_s[...] = grad_middle
    put_vec(4, col_sum(grad_middle))
    middle_low = grad_middle.astype(BF16)
    grad = dot_cols(att_s[...], middle_low).astype(BF16)
    for q in range(n_opt):
        g_ref[q, 0, 3 * part : 4 * part, :] = grad[q * part : (q + 1) * part]
    datt_s[...] = dot_rows(middle_low, wide_s[0, 3]).astype(BF16)

    def backward(i, carry):
        at = pl.ds(pl.multiple_of(i * seq_pad, 16), seq_pad)
        for p in range(pairs):
            col = slice(p * lanes, (p + 1) * lanes)
            queries, keys, values = qkv_s[0, at, col], qkv_s[1, at, col], qkv_s[2, at, col]
            datt = datt_s[at, col]
            grads = ([], [], [])
            for side in range(2):
                probs = probs_s[i, 2 * p + side]
                grads[2].append(dot_cols(probs.astype(BF16), datt))
                grad_probs = dot_rows(only(datt, side), values)
                row_dot = jnp.sum(probs * grad_probs, -1, keepdims=True)
                grad_scores = (probs * (grad_probs - row_dot) * scale).astype(BF16)
                grads[0].append(dot_plain(grad_scores, keys))
                grads[1].append(dot_cols(grad_scores, queries))
            for k in range(3):
                dqkv_s[k, at, col] = join(grads[k])
        return carry

    lax.fori_loop(0, n_img, backward, 0)
    put_vec(2, col_sum(dqkv_s[0]))
    put_vec(3, col_sum(dqkv_s[2]))
    normed_one, inv_one = norm_rows(rows_s[...])
    act_one = (normed_one * vec(0) + vec(1)).astype(BF16)
    grad_act_one = jnp.zeros_like(normed_one)
    for k in range(3):
        low = dqkv_s[k].astype(BF16)
        grad = dot_cols(act_one, low).astype(BF16)
        for q in range(n_opt):
            g_ref[q, 0, k * part : (k + 1) * part, :] = grad[q * part : (q + 1) * part]
        grad_act_one = grad_act_one + dot_rows(low, wide_s[0, k])
    put_vec(0, col_sum(grad_act_one * normed_one))
    put_vec(1, col_sum(grad_act_one))
    mid_s[...] = gmid_s[...] + norm_back(grad_act_one * vec(0), normed_one, inv_one)
    for i in range(n_img):
        gx_ref[i] = mid_s[i * seq_pad : i * seq_pad + seq_len, :].astype(BF16)


def layer_step(tokens, cotangent, weights, small, small_count):
    n_img, seq_len, width = tokens.shape
    seq_pad = seq_len + -seq_len % 16
    total = n_img * seq_pad
    heads = width // HEAD_DIM
    vmem = pl.BlockSpec(memory_space=pltpu.VMEM)
    return pl.pallas_call(
        functools.partial(layer_kernel, seq_len, seq_pad, small_count),
        out_shape=(
            jax.ShapeDtypeStruct(tokens.shape, BF16),
            jax.ShapeDtypeStruct(tokens.shape, BF16),
            jax.ShapeDtypeStruct(weights.shape, BF16),
            jax.ShapeDtypeStruct(small.shape, F32),
        ),
        in_specs=[vmem] * 4,
        out_specs=[vmem] * 4,
        scratch_shapes=[
            pltpu.VMEM((total, width), F32),
            pltpu.VMEM((total, width), F32),
            pltpu.VMEM((2, 4, width, width), BF16),
            pltpu.VMEM((3, total, width), BF16),
            pltpu.VMEM((n_img, heads, seq_pad, seq_pad), F32),
            pltpu.VMEM((total, width), BF16),
            pltpu.VMEM((total, width), BF16),
            pltpu.VMEM((3, total, width), F32),
            pltpu.VMEM((total, width), F32),
            pltpu.VMEM((total, width), F32),
        ],
        compiler_params=pltpu.CompilerParams(vmem_limit_bytes=56 * 2**20),
        name="layer_step",
    )(tokens, cotangent, weights, small)


def body(
    tokens,
    cotangent,
    w_qkv,
    w_proj,
    w_fc1,
    w_fc2,
    vectors,
    mom_qkv,
    mom_proj,
    mom_fc1,
    mom_fc2,
    mom_vectors,
):
    n_dp, n_opt = lax.axis_size("dp"), lax.axis_size("opt")
    part, width = w_proj.shape
    rows = width // n_dp
    small_count = vectors.shape[0]
    pad = -small_count % 8

    def cut(packed):
        return packed.reshape(packed.shape[:-2] + (n_dp, rows, width))

    def join(packed):
        return packed.reshape(packed.shape[:-3] + (width, width))

    weights_mine = cut(pack_rows(*[w.astype(BF16) for w in (w_qkv, w_proj, w_fc1, w_fc2)]))
    small_mine = jnp.pad(vectors.astype(BF16).astype(F32), ((0, pad), (0, 0)))
    all_weights, all_small = gather_weights(weights_mine, small_mine, n_dp, n_opt)
    all_weights = join(all_weights)
    outputs, grad_tokens, packed, small = layer_step(
        tokens, cotangent, all_weights, all_small, small_count
    )
    packed = cut(packed)
    token_total = tokens.shape[0] * tokens.shape[1] * n_dp * n_opt
    grad_scale = 1.0 / math.sqrt(token_total)
    moms = cut(pack_rows(mom_qkv, mom_proj, mom_fc1, mom_fc2))
    summed, small_sum = reduce_grads(packed, small, moms, grad_scale, n_dp, n_opt)
    summed = join(summed)
    shares = tuple(x.astype(F32) for x in unpack_rows(summed[:3], part)) + (
        small_sum[:small_count],
    )
    old_moms = (mom_qkv, mom_proj, mom_fc1, mom_fc2, mom_vectors)
    new_moms = tuple(
        (
            MOMENTUM_DECAY * old_state + share_part * grad_scale
            for old_state, share_part in zip(old_moms, shares)
        )
    )
    vector_mom = new_moms[4]
    new_vectors = vectors - VECTOR_RATE * vector_mom * lax.rsqrt(
        jnp.mean(vector_mom * vector_mom, -1, keepdims=True) + NORM_EPSILON
    )
    ortho = newton_owned(summed[3:])
    updates = join(spread_updates(cut(ortho), 3 * part // rows, n_dp, n_opt))
    new_mats = tuple(
        (
            weight_now - update_part.astype(F32)
            for weight_now, update_part in zip(
                (w_qkv, w_proj, w_fc1, w_fc2), unpack_rows(updates, part)
            )
        )
    )
    return (outputs, grad_tokens) + shares + new_mats + (new_vectors,) + new_moms


def solution(mesh):
    return jax.shard_map(
        body,
        mesh=mesh,
        in_specs=(
            P(("dp", "opt"), None, None),
            P(("dp", "opt"), None, None),
            P("opt", None),
            P("opt", None),
            P("opt", None),
            P("opt", None),
            P("opt", None),
            P("opt", None),
            P("opt", None),
            P("opt", None),
            P("opt", None),
            P("opt", None),
        ),
        out_specs=(
            P(("dp", "opt"), None, None),
            P(("dp", "opt"), None, None),
            P("opt", None),
            P("opt", None),
            P("opt", None),
            P("opt", None),
            P("opt", None),
            P("opt", None),
            P("opt", None),
            P("opt", None),
            P("opt", None),
            P("opt", None),
            P("opt", None),
            P("opt", None),
            P("opt", None),
            P("opt", None),
            P("opt", None),
        ),
        check_vma=False,
    )
```
